32 devices in a mesh: grp: 2 (over y), seq: 4 (over z), ch: 4 (over x, core).
Axes of the slice: x: 2, y: 2, z: 4, core: 2. Of those that a mesh axis runs over, the one named last changes fastest.
Arguments:
- activations: bfloat16 [4096, 1024], P('ch', ('grp', 'seq')), parts along dimension 1, may hold values from -6 to 6
- projection: bfloat16 [4096, 2048], P('seq', 'ch'), may hold values from -0.09375 to 0.09375
- medium_taps: float32 [2048, 128], P('ch'), may hold values from -0.5 to 0.5
- long_filters: bfloat16 [2048, 512], P('ch', 'seq'), may hold values from -0.25 to 0.25
- cotangent: bfloat16 [2048, 1024], P('ch', ('grp', 'seq')), parts along dimension 1, may hold values from -6 to 6
Outputs:
- conv_out: bfloat16 [2048, 1024], P('ch', ('grp', 'seq')), parts along dimension 1
- input_grad: bfloat16 [4096, 1024], P('ch', ('grp', 'seq')), parts along dimension 1
The draws below stay inside these ranges and needn't reach their ends.
There are 2 independent parts, one for each index of `grp`. The reference program is written for one: setup_inputs(seed, part) draws one part's arguments, and reference() takes and returns one part's arrays. A program takes and returns all parts, laid end to end along the dimension named above; an argument that names none is the same for every part. Nothing has to cross between parts.
All inputs are finite; a program needn't handle non-finite values.
Results may differ from the reference program's by a relative error of at most 0.012.
Values may be sent and summed in bfloat16 or wider, within the bound.
A program may use at most 64 MiB of HBM per device.

```python
import jax
import jax.numpy as jnp
from jax import lax

D = 4096
C = 2048
K = 128
LENGTH = 512


def block_scale(rng, dims, split, smallest, top_value):
    factor_of, own = 1.0, jax.random.fold_in(rng, 6)
    for axis_at, shards_of in split:
        draws = jnp.exp(jax.random.uniform(jax.random.fold_in(own, axis_at), (shards_of,), jnp.float32, smallest / len(split), top_value / len(split)))
        factor_of = factor_of * jnp.repeat(draws, dims[axis_at] // shards_of).reshape([-1 if axis == axis_at else 1 for axis in range(len(dims))])
    return factor_of


def gaussian(own_key, extent, spread, bound, cuts=(), dtype=jnp.bfloat16):
    entries = spread * jax.random.normal(own_key, extent, jnp.float32)
    if cuts:
        entries = entries * block_scale(own_key, extent, cuts, -0.22, 0.18)
    return jnp.clip(entries, -bound, bound).astype(dtype)


def setup_inputs(seed: int = 0, part: int = 0) -> dict:
    splits = jax.random.split(jax.random.key(seed), 6)
    own_keys = jax.random.split(jax.random.fold_in(splits[5], part), 6)
    return {
        "activations": gaussian(own_keys[0], (D, LENGTH), 1.0, 6.0, ((0, 4), (1, 4))),
        "projection": gaussian(splits[1], (D, C), D ** -0.5, 0.09375, ((0, 4), (1, 4))),
        "medium_taps": gaussian(splits[2], (C, K), K ** -0.5, 0.5, ((0, 4),), jnp.float32),
        "long_filters": gaussian(splits[3], (C, LENGTH), LENGTH ** -0.5, 0.25, ((0, 4), (1, 4))),
        "cotangent": gaussian(own_keys[4], (C, LENGTH), 1.0, 6.0, ((0, 4), (1, 4))),
    }


def medium_forward(padded, tap_weights, length):
    tap_count = tap_weights.shape[1]
    summed = jnp.zeros((padded.shape[0], length), jnp.float32)
    for offset in range(tap_count):
        begin_col = tap_count - 1 - offset
        summed = summed + tap_weights[:, offset:offset + 1] * padded[:, begin_col:begin_col + length]
    return summed


def medium_backward(padded, tap_weights, length):
    tap_count = tap_weights.shape[1]
    summed = jnp.zeros((padded.shape[0], length), jnp.float32)
    for offset in range(tap_count):
        summed = summed + tap_weights[:, offset:offset + 1] * padded[:, offset:offset + length]
    return summed


def long_apply(signal, filter_row, conjugate):
    length = signal.shape[-1]
    points = 2 * length
    sig_spec = jnp.fft.rfft(signal, n=points, axis=-1)
    filt_spec = jnp.fft.rfft(filter_row, n=points, axis=-1)
    if conjugate:
        filt_spec = jnp.conj(filt_spec)
    return jnp.fft.irfft(sig_spec * filt_spec, n=points, axis=-1)[..., :length]


def long_blocks(signal, filters, conjugate):
    channels, length = signal.shape

    def run_block(operands):
        return long_apply(operands[0], operands[1], conjugate)

    result = lax.map(run_block, (signal.reshape(channels // 128, 128, length), filters.reshape(channels // 128, 128, length)))
    return result.reshape(channels, length)


def reference(activations, projection, medium_taps, long_filters, cotangent):
    tap_count = medium_taps.shape[1]
    length = activations.shape[1]
    values = jnp.dot(projection.T, activations, preferred_element_type=jnp.float32).astype(jnp.bfloat16)
    values_wide = values.astype(jnp.float32)
    gate_open = jax.nn.sigmoid(values_wide)
    medium = medium_forward(jnp.pad(values_wide, ((0, 0), (tap_count - 1, 0))), medium_taps, length)
    gated_conv = lax.optimization_barrier((medium * gate_open).astype(jnp.bfloat16))
    filters_wide = long_filters.astype(jnp.float32)
    conv_out = long_blocks(gated_conv.astype(jnp.float32), filters_wide, False).astype(jnp.bfloat16)
    grad_gated = lax.optimization_barrier(long_blocks(cotangent.astype(jnp.float32), filters_wide, True).astype(jnp.bfloat16))
    grad_wide = grad_gated.astype(jnp.float32)
    grad_medium = lax.optimization_barrier((grad_wide * gate_open).astype(jnp.bfloat16)).astype(jnp.float32)
    through = medium_backward(jnp.pad(grad_medium, ((0, 0), (0, tap_count - 1))), medium_taps, length)
    grad_values = (through + grad_wide * medium * gate_open * (1.0 - gate_open)).astype(jnp.bfloat16)
    input_grad = jnp.dot(projection, grad_values, preferred_element_type=jnp.float32).astype(jnp.bfloat16)
    return conv_out, input_grad
```

```python
import functools
import math

import jax
import jax.numpy as jnp
import numpy as np
from jax import lax
from jax.experimental import pallas as pl
from jax.experimental.pallas import tpu as pltpu
from jax.sharding import PartitionSpec as P

exact_mode = lax.Precision.HIGH


def medium_forward(padded, tap_weights, length):
    tap_count = tap_weights.shape[1]
    summed = jnp.zeros((padded.shape[0], length), jnp.float32)
    for offset in range(tap_count):
        begin_col = tap_count - 1 - offset
        summed = (
            summed + tap_weights[:, offset : offset + 1] * padded[:, begin_col : begin_col + length]
        )
    return summed


def medium_backward(padded, tap_weights, length):
    tap_count = tap_weights.shape[1]
    summed = jnp.zeros((padded.shape[0], length), jnp.float32)
    for offset in range(tap_count):
        summed = summed + tap_weights[:, offset : offset + 1] * padded[:, offset : offset + length]
    return summed


def dft_tables(length):
    points = 2 * length
    columns = 128
    row_count = points // columns
    half_rows = row_count // 2
    freq_rows = jnp.arange(row_count, dtype=jnp.int32)
    time_rows = jnp.arange(half_rows, dtype=jnp.int32)
    lane_index = jnp.arange(columns, dtype=jnp.int32)
    angle_first = (
        2.0
        * math.pi
        / row_count
        * (freq_rows[:, None] * time_rows[None, :] % row_count).astype(jnp.float32)
    )
    angle_twist = (
        2.0
        * math.pi
        / points
        * (freq_rows[:, None] * lane_index[None, :] % points).astype(jnp.float32)
    )
    angle_last = (
        2.0
        * math.pi
        / columns
        * (lane_index[:, None] * lane_index[None, :] % columns).astype(jnp.float32)
    )
    return (
        jnp.cos(angle_first),
        jnp.sin(angle_first),
        jnp.cos(angle_twist),
        jnp.sin(angle_twist),
        jnp.cos(angle_last),
        jnp.sin(angle_last),
    )


def forward_dft(signal, tables):
    cos_first, sin_first, cos_twist, sin_twist, cos_last, sin_last = tables
    channels = signal.shape[0]
    shaped = signal.reshape(channels, cos_first.shape[1], 128)
    section_re = jnp.einsum("kn,cnq->ckq", cos_first, shaped, precision=exact_mode)
    section_im = -jnp.einsum("kn,cnq->ckq", sin_first, shaped, precision=exact_mode)
    twist_re = section_re * cos_twist + section_im * sin_twist
    twist_im = section_im * cos_twist - section_re * sin_twist
    spec_re = jnp.einsum("ckq,qm->ckm", twist_re, cos_last, precision=exact_mode) + jnp.einsum(
        "ckq,qm->ckm", twist_im, sin_last, precision=exact_mode
    )
    spec_im = jnp.einsum("ckq,qm->ckm", twist_im, cos_last, precision=exact_mode) - jnp.einsum(
        "ckq,qm->ckm", twist_re, sin_last, precision=exact_mode
    )
    return (spec_re, spec_im)


def inverse_dft(spec_re, spec_im, tables):
    cos_first, sin_first, cos_twist, sin_twist, cos_last, sin_last = tables
    channels = spec_re.shape[0]
    half_rows = cos_first.shape[1]
    inner_re = jnp.einsum("ckq,qm->ckm", spec_re, cos_last, precision=exact_mode) - jnp.einsum(
        "ckq,qm->ckm", spec_im, sin_last, precision=exact_mode
    )
    inner_im = jnp.einsum("ckq,qm->ckm", spec_im, cos_last, precision=exact_mode) + jnp.einsum(
        "ckq,qm->ckm", spec_re, sin_last, precision=exact_mode
    )
    turned_re = inner_re * cos_twist - inner_im * sin_twist
    turned_im = inner_im * cos_twist + inner_re * sin_twist
    output = jnp.einsum("kn,ckq->cnq", cos_first, turned_re, precision=exact_mode) - jnp.einsum(
        "kn,ckq->cnq", sin_first, turned_im, precision=exact_mode
    )
    points = 2 * half_rows * 128
    return (output / points).reshape(channels, half_rows * 128)


def causal_apply(signal, filt_re, filt_im, tables, conjugate):
    sig_re, sig_im = forward_dft(signal, tables)
    if conjugate:
        prod_re = sig_re * filt_re + sig_im * filt_im
        prod_im = sig_im * filt_re - sig_re * filt_im
    else:
        prod_re = sig_re * filt_re - sig_im * filt_im
        prod_im = sig_im * filt_re + sig_re * filt_im
    return inverse_dft(prod_re, prod_im, tables)


def on_device(activations, projection, medium_taps, long_filters, cotangent):
    tap_count = medium_taps.shape[1]
    whole_in = lax.all_gather(activations, "ch", axis=0, tiled=True)
    mixed_sum = lax.dot_general(
        lax.all_gather(projection, "seq", axis=0, tiled=True),
        whole_in,
        (((0,), (0,)), ((), ())),
        preferred_element_type=jnp.float32,
    )
    values = mixed_sum.astype(jnp.bfloat16)
    channel_count = values.shape[0] // lax.axis_size("seq")
    own_taps = lax.dynamic_slice_in_dim(
        medium_taps, lax.axis_index("seq") * channel_count, channel_count, 0
    )
    arrived, filters_ch = (
        lax.all_to_all(values, "seq", split_axis=0, concat_axis=1, tiled=True),
        lax.all_to_all(long_filters, "seq", split_axis=0, concat_axis=1, tiled=True),
    )
    tables = dft_tables(arrived.shape[1])
    filt_re, filt_im = forward_dft(filters_ch.astype(jnp.float32), tables)
    values_ch = arrived.astype(jnp.float32)
    padded_ch = jnp.pad(values_ch, ((0, 0), (tap_count - 1, 0)))
    conv_ch = medium_forward(padded_ch, own_taps, arrived.shape[1])
    gate_ch = jax.nn.sigmoid(values_ch)
    signal = lax.optimization_barrier((conv_ch * gate_ch).astype(jnp.bfloat16)).astype(jnp.float32)
    kept_state = (conv_ch, gate_ch)
    output_ch = causal_apply(signal, filt_re, filt_im, tables, False).astype(jnp.bfloat16)
    output_ch, context = (output_ch, (filt_re, filt_im, tables, kept_state))
    conv_out = lax.all_to_all(output_ch, "seq", split_axis=1, concat_axis=0, tiled=True)
    grad_ch = lax.all_to_all(cotangent, "seq", split_axis=0, concat_axis=1, tiled=True)
    filt_re, filt_im, tables, kept_state = context
    back_grad = lax.optimization_barrier(
        causal_apply(grad_ch.astype(jnp.float32), filt_re, filt_im, tables, True).astype(
            jnp.bfloat16
        )
    )
    conv_ch, gate_ch = kept_state
    grad_wide = back_grad.astype(jnp.float32)
    conv_grad = lax.optimization_barrier((grad_wide * gate_ch).astype(jnp.bfloat16)).astype(
        jnp.float32
    )
    padded_grad = jnp.pad(conv_grad, ((0, 0), (0, tap_count - 1)))
    through = medium_backward(padded_grad, own_taps, conv_grad.shape[1])
    gate_grad = grad_wide * conv_ch * gate_ch * (1.0 - gate_ch)
    back_ch = (through + gate_grad).astype(jnp.bfloat16)
    returned = lax.all_to_all(back_ch, "seq", split_axis=1, concat_axis=0, tiled=True)
    partial_grad = jnp.dot(
        lax.all_gather(projection, "seq", axis=0, tiled=True),
        returned,
        preferred_element_type=jnp.float32,
    )
    input_grad = lax.psum_scatter(
        partial_grad.astype(jnp.bfloat16), "ch", scatter_dimension=0, tiled=True
    )
    return (conv_out, input_grad)


MESH = pl.DeviceIdType.MESH


def transform_table(length):
    points = 2 * length
    turns = np.arange(length)[:, None] * (2 * np.arange(length)[None, :] + 1) % (2 * points)
    angles = turns * (math.pi / points)
    return jnp.asarray(np.concatenate([np.cos(angles), np.sin(angles)], axis=1), jnp.bfloat16)


def to_spectrum(signal, table):
    spectrum = jnp.dot(signal, table, preferred_element_type=jnp.float32)
    half = spectrum.shape[1] // 2
    return spectrum[:, :half], spectrum[:, half:]


def from_spectrum(even, odd, table):
    both = jnp.concatenate([even, odd], axis=1).astype(jnp.bfloat16)
    signal = lax.dot_general(
        both, table, (((1,), (1,)), ((), ())), preferred_element_type=jnp.float32
    )
    return signal * (1.0 / table.shape[0])


def times(left, right):
    return left[0] * right[0] - left[1] * right[1], left[0] * right[1] + left[1] * right[0]


def times_conj(left, right):
    return left[0] * right[0] + left[1] * right[1], left[1] * right[0] - left[0] * right[1]


def stacked(first, second):
    return (
        jnp.concatenate([first[0], second[0]], axis=0),
        jnp.concatenate([first[1], second[1]], axis=0),
    )


def fused_kernel(
    ns,
    nc,
    pieces,
    act_ref,
    proj_ref,
    taps_ref,
    filt_ref,
    cot_ref,
    table_ref,
    conv_ref,
    grad_ref,
    held_act,
    all_act,
    wide_in,
    part_sum,
    got_sum,
    conv_own,
    conv_got,
    all_grad,
    part_grad,
    pair_grad,
    mirror_send,
    mirror_got,
    total_grad,
    turned,
    grad_got,
    send_sems,
    recv_sems,
):
    s = lax.axis_index("seq")
    h = lax.axis_index("ch")
    rows = act_ref.shape[0]
    span = act_ref.shape[1]
    own = filt_ref.shape[0] // ns
    quarter = rows // nc
    piece = quarter // pieces
    length = span * ns
    partner = h + 1 - 2 * (h % 2)
    mirror = (h + nc // 2) % nc
    across = (partner + nc // 2) % nc
    started = []

    def block(index, size):
        return pl.ds(pl.multiple_of(index * size, size), size)

    def part(index, k):
        return pl.ds(pl.multiple_of(index * quarter + k * piece, piece), piece)

    def send(src, dst, **where):
        slot = len(started)
        copy = pltpu.make_async_remote_copy(
            src_ref=src,
            dst_ref=dst,
            send_sem=send_sems.at[slot],
            recv_sem=recv_sems.at[slot],
            device_id=where,
            device_id_type=MESH,
        )
        copy.start()
        started.append(copy)
        return copy

    barrier = pltpu.get_barrier_semaphore()
    for d in range(1, ns):
        pl.semaphore_signal(
            barrier, inc=1, device_id={"seq": (s + d) % ns}, device_id_type=MESH
        )
    for d in range(1, nc):
        pl.semaphore_signal(barrier, inc=1, device_id={"ch": (h + d) % nc}, device_id_type=MESH)
    pl.semaphore_wait(barrier, ns + nc - 2)

    spread = []
    for k in range(pieces):
        spread.append(
            [
                send(
                    act_ref.at[part((h + d) % nc, k), :],
                    held_act.at[h, pl.ds(k * piece, piece), :],
                    ch=(h + d) % nc,
                )
                for d in range(1, nc)
            ]
        )
    held_act[h] = act_ref[block(h, quarter), :]
    moved = []
    for k in range(pieces):
        for copy in spread[k]:
            copy.wait_recv()
        moved.append(
            [
                send(
                    held_act.at[(s + d) % ns, pl.ds(k * piece, piece), :],
                    all_act.at[part(h, k), block(s, span)],
                    seq=(s + d) % ns,
                )
                for d in range(1, ns)
            ]
        )
    all_act[block(h, quarter), block(s, span)] = held_act[s]
    wide = []
    for at, ref in enumerate((filt_ref, cot_ref)):
        for d in range(1, ns):
            wide.append(
                send(
                    ref.at[block((s + d) % ns, own), :],
                    wide_in.at[pl.ds(at * own, own), block(s, span)],
                    seq=(s + d) % ns,
                )
            )
        wide_in[pl.ds(at * own, own), block(s, span)] = ref[block(s, own), :]
    shared, crossed = [], []
    for k in range(pieces):
        for copy in moved[k]:
            copy.wait_recv()
        crossed.append(send(all_act.at[part(h, k), :], all_act.at[part(h, k), :], ch=mirror))
        shared.append(send(all_act.at[part(h, k), :], all_act.at[part(h, k), :], ch=partner))

    for copy in wide:
        copy.wait_recv()
    table = table_ref[...]
    spec = to_spectrum(wide_in[...], table)
    filt = (spec[0][:own], spec[1][:own])
    cot = (spec[0][own:], spec[1][own:])
    taps_own = taps_ref[block(s, own), :]
    taps_high = taps_own.astype(jnp.bfloat16)
    taps_low = (taps_own - taps_high.astype(jnp.float32)).astype(jnp.bfloat16)
    table_top = table_ref[pl.ds(0, taps_own.shape[1]), :]
    high = to_spectrum(taps_high, table_top)
    low = to_spectrum(taps_low, table_top)
    taps = (high[0] + low[0], high[1] + low[1])
    back = from_spectrum(*times_conj(cot, filt), table).astype(jnp.bfloat16).astype(jnp.float32)

    for k in range(pieces):
        crossed[k].wait_recv()
        shared.append(
            send(all_act.at[part(mirror, k), :], all_act.at[part(mirror, k), :], ch=partner)
        )
    for copy in shared:
        copy.wait_recv()

    summed = lax.dot_general(
        proj_ref[...],
        all_act[...],
        (((0,), (0,)), ((), ())),
        preferred_element_type=jnp.float32,
    )
    part_sum[...] = summed.astype(jnp.bfloat16)
    reduced = [
        send(
            part_sum.at[block((s + d) % ns, own), :],
            got_sum.at[d - 1],
            seq=(s + d) % ns,
        )
        for d in range(1, ns)
    ]
    mixed = part_sum[block(s, own), :].astype(jnp.float32)
    for d in range(1, ns):
        reduced[d - 1].wait_recv()
        mixed = mixed + got_sum[d - 1].astype(jnp.float32)
    values = mixed.astype(jnp.bfloat16)
    gate = jax.nn.sigmoid(values.astype(jnp.float32))
    grad_medium = (back * gate).astype(jnp.bfloat16)
    spec = to_spectrum(jnp.concatenate([values, grad_medium], axis=0), table)
    both = stacked(
        times((spec[0][:own], spec[1][:own]), taps),
        times_conj((spec[0][own:], spec[1][own:]), taps),
    )
    both = from_spectrum(*both, table)
    medium, through = both[:own], both[own:]
    all_grad[block(s, own), :] = (through + back * medium * gate * (1.0 - gate)).astype(
        jnp.bfloat16
    )
    gathered = [
        send(all_grad.at[block(s, own), :], all_grad.at[block(s, own), :], seq=(s + d) % ns)
        for d in range(1, ns)
    ]

    gated = (medium * gate).astype(jnp.bfloat16)
    conv = from_spectrum(*times(to_spectrum(gated, table), filt), table)
    conv_own[...] = conv.astype(jnp.bfloat16)
    returned = [
        send(
            conv_own.at[:, block((s + d) % ns, span)],
            conv_got.at[block(s, own), :],
            seq=(s + d) % ns,
        )
        for d in range(1, ns)
    ]
    conv_got[block(s, own), :] = conv_own[:, block(s, span)]

    for copy in gathered:
        copy.wait_recv()
    first, second = [], []
    for k in range(pieces):
        for to, copies in ((across, first), (partner, second)):
            got = jnp.dot(
                proj_ref[part(to, k), :], all_grad[...], preferred_element_type=jnp.float32
            )
            part_grad[part(to, k), :] = got.astype(jnp.bfloat16)
            side = 0 if copies is first else 1
            copies.append(
                send(
                    part_grad.at[part(to, k), :],
                    pair_grad.at[side, pl.ds(k * piece, piece), :],
                    ch=partner,
                )
            )
    mirrored = []
    for k in range(pieces):
        at = pl.ds(k * piece, piece)
        kept = jnp.dot(
            proj_ref[part(mirror, k), :], all_grad[...], preferred_element_type=jnp.float32
        )
        first[k].wait_recv()
        kept = kept + pair_grad[0, at, :].astype(jnp.float32)
        mirror_send[at, :] = kept.astype(jnp.bfloat16)
        mirrored.append(send(mirror_send.at[at, :], mirror_got.at[at, :], ch=mirror))
    placed = []
    for k in range(pieces):
        at = pl.ds(k * piece, piece)
        kept = jnp.dot(proj_ref[part(h, k), :], all_grad[...], preferred_element_type=jnp.float32)
        second[k].wait_recv()
        kept = kept + pair_grad[1, at, :].astype(jnp.float32)
        mirrored[k].wait_recv()
        kept = kept + mirror_got[at, :].astype(jnp.float32)
        total_grad[at, :] = kept.astype(jnp.bfloat16)
        placed.append(
            [
                send(
                    total_grad.at[at, block((s + d) % ns, span)],
                    turned.at[s, at, :],
                    seq=(s + d) % ns,
                )
                for d in range(1, ns)
            ]
        )
        turned[s, at, :] = total_grad[at, block(s, span)]
    final = []
    for k in range(pieces):
        at = pl.ds(k * piece, piece)
        for copy in placed[k]:
            copy.wait_recv()
        final += [
            send(turned.at[(h + d) % nc, at, :], grad_got.at[part(h, k), :], ch=(h + d) % nc)
            for d in range(1, nc)
        ]
        grad_got[part(h, k), :] = turned[h, at, :]
    for copy in returned:
        copy.wait_recv()
    conv_ref[...] = conv_got[...]
    for copy in final:
        copy.wait_recv()
    grad_ref[...] = grad_got[...]
    for copy in started:
        copy.wait_send()


def fused_on_device(ns, nc, activations, projection, medium_taps, long_filters, cotangent):
    rows, span = activations.shape
    channels = long_filters.shape[0]
    own = channels // ns
    length = span * ns
    quarter = rows // nc
    pieces = 2
    copies = 9 * pieces + 3 * pieces + 3 * pieces + 6 * pieces + 24 + 16
    vmem = pl.BlockSpec(memory_space=pltpu.VMEM)
    bf16 = jnp.bfloat16
    return pl.pallas_call(
        functools.partial(fused_kernel, ns, nc, pieces),
        out_shape=(
            jax.ShapeDtypeStruct((channels, span), bf16),
            jax.ShapeDtypeStruct((rows, span), bf16),
        ),
        in_specs=[vmem] * 6,
        out_specs=(vmem, vmem),
        scratch_shapes=[
            pltpu.VMEM((nc, quarter, span), bf16),
            pltpu.VMEM((rows, length), bf16),
            pltpu.VMEM((2 * own, length), bf16),
            pltpu.VMEM((channels, length), bf16),
            pltpu.VMEM((ns - 1, own, length), bf16),
            pltpu.VMEM((own, length), bf16),
            pltpu.VMEM((channels, span), bf16),
            pltpu.VMEM((channels, length), bf16),
            pltpu.VMEM((rows, length), bf16),
            pltpu.VMEM((2, quarter, length), bf16),
            pltpu.VMEM((quarter, length), bf16),
            pltpu.VMEM((quarter, length), bf16),
            pltpu.VMEM((quarter, length), bf16),
            pltpu.VMEM((ns, quarter, span), bf16),
            pltpu.VMEM((rows, span), bf16),
            pltpu.SemaphoreType.DMA((copies,)),
            pltpu.SemaphoreType.DMA((copies,)),
        ],
        compiler_params=pltpu.CompilerParams(
            collective_id=0, has_side_effects=True, vmem_limit_bytes=48 * 1024 * 1024
        ),
    )(activations, projection, medium_taps, long_filters, cotangent, transform_table(length))


def solution(mesh):
    ns, nc = mesh.shape["seq"], mesh.shape["ch"]

    def on_any(activations, projection, medium_taps, long_filters, cotangent):
        arrays = (activations, projection, medium_taps, long_filters, cotangent)
        table_bytes = 4 * (activations.shape[1] * ns) ** 2
        if ns == nc == 4 and table_bytes <= 4 << 20:
            return fused_on_device(ns, nc, *arrays)
        return on_device(*arrays)

    return jax.shard_map(
        on_any,
        mesh=mesh,
        in_specs=(
            P("ch", ("grp", "seq")),
            P("seq", "ch"),
            P("ch", None),
            P("ch", "seq"),
            P("ch", ("grp", "seq")),
        ),
        out_specs=(P("ch", ("grp", "seq")), P("ch", ("grp", "seq"))),
        check_vma=False,
    )
```

```python
import functools
import math

import jax
import jax.numpy as jnp
import numpy as np
from jax import lax
from jax.experimental import pallas as pl
from jax.experimental.pallas import tpu as pltpu
from jax.sharding import PartitionSpec as P

exact_mode = lax.Precision.HIGH


def medium_forward(padded, tap_weights, length):
    tap_count = tap_weights.shape[1]
    summed = jnp.zeros((padded.shape[0], length), jnp.float32)
    for offset in range(tap_count):
        begin_col = tap_count - 1 - offset
        summed = (
            summed + tap_weights[:, offset : offset + 1] * padded[:, begin_col : begin_col + length]
        )
    return summed


def medium_backward(padded, tap_weights, length):
    tap_count = tap_weights.shape[1]
    summed = jnp.zeros((padded.shape[0], length), jnp.float32)
    for offset in range(tap_count):
        summed = summed + tap_weights[:, offset : offset + 1] * padded[:, offset : offset + length]
    return summed


def dft_tables(length):
    points = 2 * length
    columns = 128
    row_count = points // columns
    half_rows = row_count // 2
    freq_rows = jnp.arange(row_count, dtype=jnp.int32)
    time_rows = jnp.arange(half_rows, dtype=jnp.int32)
    lane_index = jnp.arange(columns, dtype=jnp.int32)
    angle_first = (
        2.0
        * math.pi
        / row_count
        * (freq_rows[:, None] * time_rows[None, :] % row_count).astype(jnp.float32)
    )
    angle_twist = (
        2.0
        * math.pi
        / points
        * (freq_rows[:, None] * lane_index[None, :] % points).astype(jnp.float32)
    )
    angle_last = (
        2.0
        * math.pi
        / columns
        * (lane_index[:, None] * lane_index[None, :] % columns).astype(jnp.float32)
    )
    return (
        jnp.cos(angle_first),
        jnp.sin(angle_first),
        jnp.cos(angle_twist),
        jnp.sin(angle_twist),
        jnp.cos(angle_last),
        jnp.sin(angle_last),
    )


def forward_dft(signal, tables):
    cos_first, sin_first, cos_twist, sin_twist, cos_last, sin_last = tables
    channels = signal.shape[0]
    shaped = signal.reshape(channels, cos_first.shape[1], 128)
    section_re = jnp.einsum("kn,cnq->ckq", cos_first, shaped, precision=exact_mode)
    section_im = -jnp.einsum("kn,cnq->ckq", sin_first, shaped, precision=exact_mode)
    twist_re = section_re * cos_twist + section_im * sin_twist
    twist_im = section_im * cos_twist - section_re * sin_twist
    spec_re = jnp.einsum("ckq,qm->ckm", twist_re, cos_last, precision=exact_mode) + jnp.einsum(
        "ckq,qm->ckm", twist_im, sin_last, precision=exact_mode
    )
    spec_im = jnp.einsum("ckq,qm->ckm", twist_im, cos_last, precision=exact_mode) - jnp.einsum(
        "ckq,qm->ckm", twist_re, sin_last, precision=exact_mode
    )
    return (spec_re, spec_im)


def inverse_dft(spec_re, spec_im, tables):
    cos_first, sin_first, cos_twist, sin_twist, cos_last, sin_last = tables
    channels = spec_re.shape[0]
    half_rows = cos_first.shape[1]
    inner_re = jnp.einsum("ckq,qm->ckm", spec_re, cos_last, precision=exact_mode) - jnp.einsum(
        "ckq,qm->ckm", spec_im, sin_last, precision=exact_mode
    )
    inner_im = jnp.einsum("ckq,qm->ckm", spec_im, cos_last, precision=exact_mode) + jnp.einsum(
        "ckq,qm->ckm", spec_re, sin_last, precision=exact_mode
    )
    turned_re = inner_re * cos_twist - inner_im * sin_twist
    turned_im = inner_im * cos_twist + inner_re * sin_twist
    output = jnp.einsum("kn,ckq->cnq", cos_first, turned_re, precision=exact_mode) - jnp.einsum(
        "kn,ckq->cnq", sin_first, turned_im, precision=exact_mode
    )
    points = 2 * half_rows * 128
    return (output / points).reshape(channels, half_rows * 128)


def causal_apply(signal, filt_re, filt_im, tables, conjugate):
    sig_re, sig_im = forward_dft(signal, tables)
    if conjugate:
        prod_re = sig_re * filt_re + sig_im * filt_im
        prod_im = sig_im * filt_re - sig_re * filt_im
    else:
        prod_re = sig_re * filt_re - sig_im * filt_im
        prod_im = sig_im * filt_re + sig_re * filt_im
    return inverse_dft(prod_re, prod_im, tables)


def on_device(activations, projection, medium_taps, long_filters, cotangent):
    tap_count = medium_taps.shape[1]
    whole_in = lax.all_gather(activations, "ch", axis=0, tiled=True)
    mixed_sum = lax.dot_general(
        lax.all_gather(projection, "seq", axis=0, tiled=True),
        whole_in,
        (((0,), (0,)), ((), ())),
        preferred_element_type=jnp.float32,
    )
    values = mixed_sum.astype(jnp.bfloat16)
    channel_count = values.shape[0] // lax.axis_size("seq")
    own_taps = lax.dynamic_slice_in_dim(
        medium_taps, lax.axis_index("seq") * channel_count, channel_count, 0
    )
    arrived, filters_ch = (
        lax.all_to_all(values, "seq", split_axis=0, concat_axis=1, tiled=True),
        lax.all_to_all(long_filters, "seq", split_axis=0, concat_axis=1, tiled=True),
    )
    tables = dft_tables(arrived.shape[1])
    filt_re, filt_im = forward_dft(filters_ch.astype(jnp.float32), tables)
    values_ch = arrived.astype(jnp.float32)
    padded_ch = jnp.pad(values_ch, ((0, 0), (tap_count - 1, 0)))
    conv_ch = medium_forward(padded_ch, own_taps, arrived.shape[1])
    gate_ch = jax.nn.sigmoid(values_ch)
    signal = lax.optimization_barrier((conv_ch * gate_ch).astype(jnp.bfloat16)).astype(jnp.float32)
    kept_state = (conv_ch, gate_ch)
    output_ch = causal_apply(signal, filt_re, filt_im, tables, False).astype(jnp.bfloat16)
    output_ch, context = (output_ch, (filt_re, filt_im, tables, kept_state))
    conv_out = lax.all_to_all(output_ch, "seq", split_axis=1, concat_axis=0, tiled=True)
    grad_ch = lax.all_to_all(cotangent, "seq", split_axis=0, concat_axis=1, tiled=True)
    filt_re, filt_im, tables, kept_state = context
    back_grad = lax.optimization_barrier(
        causal_apply(grad_ch.astype(jnp.float32), filt_re, filt_im, tables, True).astype(
            jnp.bfloat16
        )
    )
    conv_ch, gate_ch = kept_state
    grad_wide = back_grad.astype(jnp.float32)
    conv_grad = lax.optimization_barrier((grad_wide * gate_ch).astype(jnp.bfloat16)).astype(
        jnp.float32
    )
    padded_grad = jnp.pad(conv_grad, ((0, 0), (0, tap_count - 1)))
    through = medium_backward(padded_grad, own_taps, conv_grad.shape[1])
    gate_grad = grad_wide * conv_ch * gate_ch * (1.0 - gate_ch)
    back_ch = (through + gate_grad).astype(jnp.bfloat16)
    returned = lax.all_to_all(back_ch, "seq", split_axis=1, concat_axis=0, tiled=True)
    partial_grad = jnp.dot(
        lax.all_gather(projection, "seq", axis=0, tiled=True),
        returned,
        preferred_element_type=jnp.float32,
    )
    input_grad = lax.psum_scatter(
        partial_grad.astype(jnp.bfloat16), "ch", scatter_dimension=0, tiled=True
    )
    return (conv_out, input_grad)


MESH = pl.DeviceIdType.MESH


def transform_table(length):
    points = 2 * length
    turns = np.arange(length)[:, None] * (2 * np.arange(length)[None, :] + 1) % (2 * points)
    angles = turns * (math.pi / points)
    return jnp.asarray(np.concatenate([np.cos(angles), np.sin(angles)], axis=1), jnp.bfloat16)


def to_spectrum(signal, table):
    spectrum = jnp.dot(signal, table, preferred_element_type=jnp.float32)
    half = spectrum.shape[1] // 2
    return spectrum[:, :half], spectrum[:, half:]


def from_spectrum(even, odd, table):
    both = jnp.concatenate([even, odd], axis=1).astype(jnp.bfloat16)
    signal = lax.dot_general(
        both, table, (((1,), (1,)), ((), ())), preferred_element_type=jnp.float32
    )
    return signal * (1.0 / table.shape[0])


def times(left, right):
    return left[0] * right[0] - left[1] * right[1], left[0] * right[1] + left[1] * right[0]


def times_conj(left, right):
    return left[0] * right[0] + left[1] * right[1], left[1] * right[0] - left[0] * right[1]


def stacked(first, second):
    return (
        jnp.concatenate([first[0], second[0]], axis=0),
        jnp.concatenate([first[1], second[1]], axis=0),
    )


def fused_kernel(
    ns,
    nc,
    pieces,
    act_ref,
    proj_ref,
    taps_ref,
    filt_ref,
    cot_ref,
    table_ref,
    conv_ref,
    grad_ref,
    held_act,
    all_act,
    wide_in,
    part_sum,
    got_sum,
    conv_own,
    conv_got,
    all_grad,
    part_grad,
    pair_grad,
    mirror_send,
    mirror_got,
    total_grad,
    turned,
    grad_got,
    proj_v,
    proj_t,
    taps_v,
    table_v,
    send_sems,
    recv_sems,
    load_sems,
):
    s = lax.axis_index("seq")
    h = lax.axis_index("ch")
    rows = act_ref.shape[0]
    span = act_ref.shape[1]
    own = filt_ref.shape[0] // ns
    quarter = rows // nc
    piece = quarter // pieces
    length = span * ns
    partner = h + 1 - 2 * (h % 2)
    mirror = (h + nc // 2) % nc
    across = (partner + nc // 2) % nc
    started, loads = [], []
    half = own // 2

    def block(index, size):
        return pl.ds(pl.multiple_of(index * size, size), size)

    def part(index, k):
        return pl.ds(pl.multiple_of(index * quarter + k * piece, piece), piece)

    def send(src, dst, **where):
        slot = len(started)
        copy = pltpu.make_async_remote_copy(
            src_ref=src,
            dst_ref=dst,
            send_sem=send_sems.at[slot],
            recv_sem=recv_sems.at[slot],
            device_id=where,
            device_id_type=MESH,
        )
        copy.start()
        started.append(copy)
        return copy

    def load(src, dst):
        copy = pltpu.make_async_copy(src, dst, load_sems.at[len(loads)])
        copy.start()
        loads.append(copy)
        return copy

    barrier = pltpu.get_barrier_semaphore()
    for d in range(1, ns):
        pl.semaphore_signal(
            barrier, inc=1, device_id={"seq": (s + d) % ns}, device_id_type=MESH
        )
    for d in range(1, nc):
        pl.semaphore_signal(barrier, inc=1, device_id={"ch": (h + d) % nc}, device_id_type=MESH)
    act_own = load(act_ref.at[block(h, quarter), :], held_act.at[h])
    wide_own = [
        load(ref.at[block(s, own), :], wide_in.at[pl.ds(at * own, own), block(s, span)])
        for at, ref in enumerate((filt_ref, cot_ref))
    ]
    rest = [
        load(table_ref, table_v),
        load(taps_ref.at[block(s, own), :], taps_v),
        load(proj_ref, proj_v),
    ]
    pl.semaphore_wait(barrier, ns + nc - 2)

    spread = []
    for k in range(pieces):
        spread.append(
            [
                send(
                    act_ref.at[part((h + d) % nc, k), :],
                    held_act.at[h, pl.ds(k * piece, piece), :],
                    ch=(h + d) % nc,
                )
                for d in range(1, nc)
            ]
        )
    act_own.wait()
    moved = []
    for k in range(pieces):
        for copy in spread[k]:
            copy.wait_recv()
        moved.append(
            [
                send(
                    held_act.at[(s + d) % ns, pl.ds(k * piece, piece), :],
                    all_act.at[part(h, k), block(s, span)],
                    seq=(s + d) % ns,
                )
                for d in range(1, ns)
            ]
        )
    all_act[block(h, quarter), block(s, span)] = held_act[s]
    wide = []
    for at, ref in enumerate((filt_ref, cot_ref)):
        for d in range(1, ns):
            wide.append(
                send(
                    ref.at[block((s + d) % ns, own), :],
                    wide_in.at[pl.ds(at * own, own), block(s, span)],
                    seq=(s + d) % ns,
                )
            )
    shared, crossed = [], []
    for k in range(pieces):
        for copy in moved[k]:
            copy.wait_recv()
        crossed.append(send(all_act.at[part(h, k), :], all_act.at[part(h, k), :], ch=mirror))
        shared.append(send(all_act.at[part(h, k), :], all_act.at[part(h, k), :], ch=partner))

    for copy in rest:
        copy.wait()
    for at in range(ns):
        proj_t[pl.ds(at * own, own), :] = proj_v[:, pl.ds(at * own, own)].T
    for copy in wide_own:
        copy.wait()
    for copy in wide:
        copy.wait_recv()
    table = table_v[...]
    spec = to_spectrum(wide_in[...], table)
    filt = (spec[0][:own], spec[1][:own])
    cot = (spec[0][own:], spec[1][own:])
    taps_own = taps_v[...]
    taps_high = taps_own.astype(jnp.bfloat16)
    taps_low = (taps_own - taps_high.astype(jnp.float32)).astype(jnp.bfloat16)
    table_top = table_v[pl.ds(0, taps_own.shape[1]), :]
    high = to_spectrum(taps_high, table_top)
    low = to_spectrum(taps_low, table_top)
    taps = (high[0] + low[0], high[1] + low[1])
    back = from_spectrum(*times_conj(cot, filt), table).astype(jnp.bfloat16).astype(jnp.float32)

    for k in range(pieces):
        crossed[k].wait_recv()
        shared.append(
            send(all_act.at[part(mirror, k), :], all_act.at[part(mirror, k), :], ch=partner)
        )
    for copy in shared:
        copy.wait_recv()

    def half_of(index, c):
        return pl.ds(pl.multiple_of(index * own + c * half, half), half)

    def sum_to(d, c):
        return send(
            part_sum.at[half_of((s + d) % ns, c), :],
            got_sum.at[d - 1, pl.ds(c * half, half), :],
            seq=(s + d) % ns,
        )

    reduced = [[], []]
    for d in range(1, ns):
        got = jnp.dot(
            proj_t[block((s + d) % ns, own), :],
            all_act[...],
            preferred_element_type=jnp.float32,
        )
        part_sum[block((s + d) % ns, own), :] = got.astype(jnp.bfloat16)
        reduced[0].append(sum_to(d, 0))
    for d in range(1, ns):
        reduced[1].append(sum_to(d, 1))
    mixed = jnp.dot(
        proj_t[block(s, own), :], all_act[...], preferred_element_type=jnp.float32
    )
    gathered, mediums, gates = [], [], []
    for c in range(2):
        at = slice(c * half, (c + 1) * half)
        summed = mixed[at]
        for d in range(1, ns):
            reduced[c][d - 1].wait_recv()
            summed = summed + got_sum[d - 1, pl.ds(c * half, half), :].astype(jnp.float32)
        values = summed.astype(jnp.bfloat16)
        gate = jax.nn.sigmoid(values.astype(jnp.float32))
        grad_medium = (back[at] * gate).astype(jnp.bfloat16)
        spec = to_spectrum(jnp.concatenate([values, grad_medium], axis=0), table)
        taps_half = (taps[0][at], taps[1][at])
        both = stacked(
            times((spec[0][:half], spec[1][:half]), taps_half),
            times_conj((spec[0][half:], spec[1][half:]), taps_half),
        )
        both = from_spectrum(*both, table)
        medium, through = both[:half], both[half:]
        all_grad[half_of(s, c), :] = (
            through + back[at] * medium * gate * (1.0 - gate)
        ).astype(jnp.bfloat16)
        gathered += [
            send(all_grad.at[half_of(s, c), :], all_grad.at[half_of(s, c), :], seq=(s + d) % ns)
            for d in range(1, ns)
        ]
        mediums.append(medium)
        gates.append(gate)
    medium, gate = jnp.concatenate(mediums, axis=0), jnp.concatenate(gates, axis=0)

    gated = (medium * gate).astype(jnp.bfloat16)
    conv = from_spectrum(*times(to_spectrum(gated, table), filt), table)
    conv_own[...] = conv.astype(jnp.bfloat16)
    returned = [
        send(
            conv_own.at[:, block((s + d) % ns, span)],
            conv_got.at[block(s, own), :],
            seq=(s + d) % ns,
        )
        for d in range(1, ns)
    ]
    conv_got[block(s, own), :] = conv_own[:, block(s, span)]

    for copy in gathered:
        copy.wait_recv()
    first, second = [], []
    for k in range(pieces):
        for to, copies in ((across, first), (partner, second)):
            got = jnp.dot(
                proj_v[part(to, k), :], all_grad[...], preferred_element_type=jnp.float32
            )
            part_grad[part(to, k), :] = got.astype(jnp.bfloat16)
            side = 0 if copies is first else 1
            copies.append(
                send(
                    part_grad.at[part(to, k), :],
                    pair_grad.at[side, pl.ds(k * piece, piece), :],
                    ch=partner,
                )
            )
    mirrored = []
    for k in range(pieces):
        at = pl.ds(k * piece, piece)
        kept = jnp.dot(
            proj_v[part(mirror, k), :], all_grad[...], preferred_element_type=jnp.float32
        )
        first[k].wait_recv()
        kept = kept + pair_grad[0, at, :].astype(jnp.float32)
        mirror_send[at, :] = kept.astype(jnp.bfloat16)
        mirrored.append(send(mirror_send.at[at, :], mirror_got.at[at, :], ch=mirror))
    placed = []
    for k in range(pieces):
        at = pl.ds(k * piece, piece)
        kept = jnp.dot(proj_v[part(h, k), :], all_grad[...], preferred_element_type=jnp.float32)
        second[k].wait_recv()
        kept = kept + pair_grad[1, at, :].astype(jnp.float32)
        mirrored[k].wait_recv()
        kept = kept + mirror_got[at, :].astype(jnp.float32)
        total_grad[at, :] = kept.astype(jnp.bfloat16)
        placed.append(
            [
                send(
                    total_grad.at[at, block((s + d) % ns, span)],
                    turned.at[s, at, :],
                    seq=(s + d) % ns,
                )
                for d in range(1, ns)
            ]
        )
        turned[s, at, :] = total_grad[at, block(s, span)]
    final = []
    for k in range(pieces):
        at = pl.ds(k * piece, piece)
        for copy in placed[k]:
            copy.wait_recv()
        final += [
            send(turned.at[(h + d) % nc, at, :], grad_got.at[part(h, k), :], ch=(h + d) % nc)
            for d in range(1, nc)
        ]
        grad_got[part(h, k), :] = turned[h, at, :]
    for copy in returned:
        copy.wait_recv()
    conv_ref[...] = conv_got[...]
    for copy in final:
        copy.wait_recv()
    grad_ref[...] = grad_got[...]
    for copy in started:
        copy.wait_send()


def fused_on_device(ns, nc, activations, projection, medium_taps, long_filters, cotangent):
    rows, span = activations.shape
    channels = long_filters.shape[0]
    own = channels // ns
    taps = medium_taps.shape[1]
    length = span * ns
    quarter = rows // nc
    pieces = 2
    copies = 9 * pieces + 3 * pieces + 3 * pieces + 6 * pieces + 24 + 16
    vmem = pl.BlockSpec(memory_space=pltpu.VMEM)
    hbm = pl.BlockSpec(memory_space=pltpu.HBM)
    bf16 = jnp.bfloat16
    return pl.pallas_call(
        functools.partial(fused_kernel, ns, nc, pieces),
        out_shape=(
            jax.ShapeDtypeStruct((channels, span), bf16),
            jax.ShapeDtypeStruct((rows, span), bf16),
        ),
        in_specs=[hbm] * 6,
        out_specs=(vmem, vmem),
        scratch_shapes=[
            pltpu.VMEM((nc, quarter, span), bf16),
            pltpu.VMEM((rows, length), bf16),
            pltpu.VMEM((2 * own, length), bf16),
            pltpu.VMEM((channels, length), bf16),
            pltpu.VMEM((ns - 1, own, length), bf16),
            pltpu.VMEM((own, length), bf16),
            pltpu.VMEM((channels, span), bf16),
            pltpu.VMEM((channels, length), bf16),
            pltpu.VMEM((rows, length), bf16),
            pltpu.VMEM((2, quarter, length), bf16),
            pltpu.VMEM((quarter, length), bf16),
            pltpu.VMEM((quarter, length), bf16),
            pltpu.VMEM((quarter, length), bf16),
            pltpu.VMEM((ns, quarter, span), bf16),
            pltpu.VMEM((rows, span), bf16),
            pltpu.VMEM((rows, channels), bf16),
            pltpu.VMEM((channels, rows), bf16),
            pltpu.VMEM((own, taps), jnp.float32),
            pltpu.VMEM((length, 2 * length), bf16),
            pltpu.SemaphoreType.DMA((copies,)),
            pltpu.SemaphoreType.DMA((copies,)),
            pltpu.SemaphoreType.DMA((8,)),
        ],
        compiler_params=pltpu.CompilerParams(
            collective_id=0, has_side_effects=True, vmem_limit_bytes=48 * 1024 * 1024
        ),
    )(activations, projection, medium_taps, long_filters, cotangent, transform_table(length))


def solution(mesh):
    ns, nc = mesh.shape["seq"], mesh.shape["ch"]

    def on_any(activations, projection, medium_taps, long_filters, cotangent):
        arrays = (activations, projection, medium_taps, long_filters, cotangent)
        table_bytes = 4 * (activations.shape[1] * ns) ** 2
        if ns == nc == 4 and table_bytes <= 4 << 20:
            return fused_on_device(ns, nc, *arrays)
        return on_device(*arrays)

    return jax.shard_map(
        on_any,
        mesh=mesh,
        in_specs=(
            P("ch", ("grp", "seq")),
            P("seq", "ch"),
            P("ch", None),
            P("ch", "seq"),
            P("ch", ("grp", "seq")),
        ),
        out_specs=(P("ch", ("grp", "seq")), P("ch", ("grp", "seq"))),
        check_vma=False,
    )
```

```python
import functools
import math

import jax
import jax.numpy as jnp
import numpy as np
from jax import lax
from jax.experimental import pallas as pl
from jax.experimental.pallas import tpu as pltpu
from jax.sharding import PartitionSpec as P

exact_mode = lax.Precision.HIGH


def medium_forward(padded, tap_weights, length):
    tap_count = tap_weights.shape[1]
    summed = jnp.zeros((padded.shape[0], length), jnp.float32)
    for offset in range(tap_count):
        begin_col = tap_count - 1 - offset
        summed = (
            summed + tap_weights[:, offset : offset + 1] * padded[:, begin_col : begin_col + length]
        )
    return summed


def medium_backward(padded, tap_weights, length):
    tap_count = tap_weights.shape[1]
    summed = jnp.zeros((padded.shape[0], length), jnp.float32)
    for offset in range(tap_count):
        summed = summed + tap_weights[:, offset : offset + 1] * padded[:, offset : offset + length]
    return summed


def dft_tables(length):
    points = 2 * length
    columns = 128
    row_count = points // columns
    half_rows = row_count // 2
    freq_rows = jnp.arange(row_count, dtype=jnp.int32)
    time_rows = jnp.arange(half_rows, dtype=jnp.int32)
    lane_index = jnp.arange(columns, dtype=jnp.int32)
    angle_first = (
        2.0
        * math.pi
        / row_count
        * (freq_rows[:, None] * time_rows[None, :] % row_count).astype(jnp.float32)
    )
    angle_twist = (
        2.0
        * math.pi
        / points
        * (freq_rows[:, None] * lane_index[None, :] % points).astype(jnp.float32)
    )
    angle_last = (
        2.0
        * math.pi
        / columns
        * (lane_index[:, None] * lane_index[None, :] % columns).astype(jnp.float32)
    )
    return (
        jnp.cos(angle_first),
        jnp.sin(angle_first),
        jnp.cos(angle_twist),
        jnp.sin(angle_twist),
        jnp.cos(angle_last),
        jnp.sin(angle_last),
    )


def forward_dft(signal, tables):
    cos_first, sin_first, cos_twist, sin_twist, cos_last, sin_last = tables
    channels = signal.shape[0]
    shaped = signal.reshape(channels, cos_first.shape[1], 128)
    section_re = jnp.einsum("kn,cnq->ckq", cos_first, shaped, precision=exact_mode)
    section_im = -jnp.einsum("kn,cnq->ckq", sin_first, shaped, precision=exact_mode)
    twist_re = section_re * cos_twist + section_im * sin_twist
    twist_im = section_im * cos_twist - section_re * sin_twist
    spec_re = jnp.einsum("ckq,qm->ckm", twist_re, cos_last, precision=exact_mode) + jnp.einsum(
        "ckq,qm->ckm", twist_im, sin_last, precision=exact_mode
    )
    spec_im = jnp.einsum("ckq,qm->ckm", twist_im, cos_last, precision=exact_mode) - jnp.einsum(
        "ckq,qm->ckm", twist_re, sin_last, precision=exact_mode
    )
    return (spec_re, spec_im)


def inverse_dft(spec_re, spec_im, tables):
    cos_first, sin_first, cos_twist, sin_twist, cos_last, sin_last = tables
    channels = spec_re.shape[0]
    half_rows = cos_first.shape[1]
    inner_re = jnp.einsum("ckq,qm->ckm", spec_re, cos_last, precision=exact_mode) - jnp.einsum(
        "ckq,qm->ckm", spec_im, sin_last, precision=exact_mode
    )
    inner_im = jnp.einsum("ckq,qm->ckm", spec_im, cos_last, precision=exact_mode) + jnp.einsum(
        "ckq,qm->ckm", spec_re, sin_last, precision=exact_mode
    )
    turned_re = inner_re * cos_twist - inner_im * sin_twist
    turned_im = inner_im * cos_twist + inner_re * sin_twist
    output = jnp.einsum("kn,ckq->cnq", cos_first, turned_re, precision=exact_mode) - jnp.einsum(
        "kn,ckq->cnq", sin_first, turned_im, precision=exact_mode
    )
    points = 2 * half_rows * 128
    return (output / points).reshape(channels, half_rows * 128)


def causal_apply(signal, filt_re, filt_im, tables, conjugate):
    sig_re, sig_im = forward_dft(signal, tables)
    if conjugate:
        prod_re = sig_re * filt_re + sig_im * filt_im
        prod_im = sig_im * filt_re - sig_re * filt_im
    else:
        prod_re = sig_re * filt_re - sig_im * filt_im
        prod_im = sig_im * filt_re + sig_re * filt_im
    return inverse_dft(prod_re, prod_im, tables)


def on_device(activations, projection, medium_taps, long_filters, cotangent):
    tap_count = medium_taps.shape[1]
    whole_in = lax.all_gather(activations, "ch", axis=0, tiled=True)
    mixed_sum = lax.dot_general(
        lax.all_gather(projection, "seq", axis=0, tiled=True),
        whole_in,
        (((0,), (0,)), ((), ())),
        preferred_element_type=jnp.float32,
    )
    values = mixed_sum.astype(jnp.bfloat16)
    channel_count = values.shape[0] // lax.axis_size("seq")
    own_taps = lax.dynamic_slice_in_dim(
        medium_taps, lax.axis_index("seq") * channel_count, channel_count, 0
    )
    arrived, filters_ch = (
        lax.all_to_all(values, "seq", split_axis=0, concat_axis=1, tiled=True),
        lax.all_to_all(long_filters, "seq", split_axis=0, concat_axis=1, tiled=True),
    )
    tables = dft_tables(arrived.shape[1])
    filt_re, filt_im = forward_dft(filters_ch.astype(jnp.float32), tables)
    values_ch = arrived.astype(jnp.float32)
    padded_ch = jnp.pad(values_ch, ((0, 0), (tap_count - 1, 0)))
    conv_ch = medium_forward(padded_ch, own_taps, arrived.shape[1])
    gate_ch = jax.nn.sigmoid(values_ch)
    signal = lax.optimization_barrier((conv_ch * gate_ch).astype(jnp.bfloat16)).astype(jnp.float32)
    kept_state = (conv_ch, gate_ch)
    output_ch = causal_apply(signal, filt_re, filt_im, tables, False).astype(jnp.bfloat16)
    output_ch, context = (output_ch, (filt_re, filt_im, tables, kept_state))
    conv_out = lax.all_to_all(output_ch, "seq", split_axis=1, concat_axis=0, tiled=True)
    grad_ch = lax.all_to_all(cotangent, "seq", split_axis=0, concat_axis=1, tiled=True)
    filt_re, filt_im, tables, kept_state = context
    back_grad = lax.optimization_barrier(
        causal_apply(grad_ch.astype(jnp.float32), filt_re, filt_im, tables, True).astype(
            jnp.bfloat16
        )
    )
    conv_ch, gate_ch = kept_state
    grad_wide = back_grad.astype(jnp.float32)
    conv_grad = lax.optimization_barrier((grad_wide * gate_ch).astype(jnp.bfloat16)).astype(
        jnp.float32
    )
    padded_grad = jnp.pad(conv_grad, ((0, 0), (0, tap_count - 1)))
    through = medium_backward(padded_grad, own_taps, conv_grad.shape[1])
    gate_grad = grad_wide * conv_ch * gate_ch * (1.0 - gate_ch)
    back_ch = (through + gate_grad).astype(jnp.bfloat16)
    returned = lax.all_to_all(back_ch, "seq", split_axis=1, concat_axis=0, tiled=True)
    partial_grad = jnp.dot(
        lax.all_gather(projection, "seq", axis=0, tiled=True),
        returned,
        preferred_element_type=jnp.float32,
    )
    input_grad = lax.psum_scatter(
        partial_grad.astype(jnp.bfloat16), "ch", scatter_dimension=0, tiled=True
    )
    return (conv_out, input_grad)


MESH = pl.DeviceIdType.MESH


def transform_table(length):
    points = 2 * length
    turns = np.arange(length)[:, None] * (2 * np.arange(length)[None, :] + 1) % (2 * points)
    angles = turns * (math.pi / points)
    return jnp.asarray(np.concatenate([np.cos(angles), np.sin(angles)], axis=1), jnp.bfloat16)


def to_spectrum(signal, table):
    spectrum = jnp.dot(signal, table, preferred_element_type=jnp.float32)
    half = spectrum.shape[1] // 2
    return spectrum[:, :half], spectrum[:, half:]


def from_spectrum(even, odd, table):
    both = jnp.concatenate([even, odd], axis=1).astype(jnp.bfloat16)
    signal = lax.dot_general(
        both, table, (((1,), (1,)), ((), ())), preferred_element_type=jnp.float32
    )
    return signal * (1.0 / table.shape[0])


def times(left, right):
    return left[0] * right[0] - left[1] * right[1], left[0] * right[1] + left[1] * right[0]


def times_conj(left, right):
    return left[0] * right[0] + left[1] * right[1], left[1] * right[0] - left[0] * right[1]


def stacked(first, second):
    return (
        jnp.concatenate([first[0], second[0]], axis=0),
        jnp.concatenate([first[1], second[1]], axis=0),
    )


def fused_kernel(
    ns,
    nc,
    pieces,
    act_ref,
    proj_ref,
    taps_ref,
    filt_ref,
    cot_ref,
    table_ref,
    conv_ref,
    grad_ref,
    held_act,
    all_act,
    wide_in,
    part_sum,
    got_sum,
    conv_own,
    conv_got,
    all_grad,
    part_grad,
    pair_grad,
    mirror_send,
    mirror_got,
    total_grad,
    turned,
    grad_got,
    proj_v,
    proj_t,
    taps_v,
    table_v,
    send_sems,
    recv_sems,
    load_sems,
):
    s = lax.axis_index("seq")
    h = lax.axis_index("ch")
    rows = act_ref.shape[0]
    span = act_ref.shape[1]
    own = filt_ref.shape[0] // ns
    quarter = rows // nc
    piece = quarter // pieces
    length = span * ns
    partner = h + 1 - 2 * (h % 2)
    mirror = (h + nc // 2) % nc
    across = (partner + nc // 2) % nc
    started, loads = [], []
    half = own // 2

    def block(index, size):
        return pl.ds(pl.multiple_of(index * size, size), size)

    def part(index, k):
        return pl.ds(pl.multiple_of(index * quarter + k * piece, piece), piece)

    def send(src, dst, **where):
        slot = len(started)
        copy = pltpu.make_async_remote_copy(
            src_ref=src,
            dst_ref=dst,
            send_sem=send_sems.at[slot],
            recv_sem=recv_sems.at[slot],
            device_id=where,
            device_id_type=MESH,
        )
        copy.start()
        started.append(copy)
        return copy

    def load(src, dst):
        copy = pltpu.make_async_copy(src, dst, load_sems.at[len(loads)])
        copy.start()
        loads.append(copy)
        return copy

    barrier = pltpu.get_barrier_semaphore()
    for d in range(1, ns):
        pl.semaphore_signal(
            barrier, inc=1, device_id={"seq": (s + d) % ns}, device_id_type=MESH
        )
    for d in range(1, nc):
        pl.semaphore_signal(barrier, inc=1, device_id={"ch": (h + d) % nc}, device_id_type=MESH)
    act_own = load(act_ref.at[block(h, quarter), :], held_act.at[h])
    wide_own = [
        load(ref.at[block(s, own), :], wide_in.at[pl.ds(at * own, own), block(s, span)])
        for at, ref in enumerate((filt_ref, cot_ref))
    ]
    rest = [
        load(table_ref, table_v),
        load(taps_ref.at[block(s, own), :], taps_v),
        load(proj_ref, proj_v),
    ]
    pl.semaphore_wait(barrier, ns + nc - 2)

    spread = []
    for k in range(pieces):
        spread.append(
            [
                send(
                    act_ref.at[part((h + d) % nc, k), :],
                    held_act.at[h, pl.ds(k * piece, piece), :],
                    ch=(h + d) % nc,
                )
                for d in range(1, nc)
            ]
        )
    act_own.wait()
    moved = []
    for k in range(pieces):
        for copy in spread[k]:
            copy.wait_recv()
        moved.append(
            [
                send(
                    held_act.at[(s + d) % ns, pl.ds(k * piece, piece), :],
                    all_act.at[part(h, k), block(s, span)],
                    seq=(s + d) % ns,
                )
                for d in range(1, ns)
            ]
        )
    all_act[block(h, quarter), block(s, span)] = held_act[s]
    wide = []
    for at, ref in enumerate((filt_ref, cot_ref)):
        for d in range(1, ns):
            wide.append(
                send(
                    ref.at[block((s + d) % ns, own), :],
                    wide_in.at[pl.ds(at * own, own), block(s, span)],
                    seq=(s + d) % ns,
                )
            )
    shared, crossed = [], []
    for k in range(pieces):
        for copy in moved[k]:
            copy.wait_recv()
        crossed.append(send(all_act.at[part(h, k), :], all_act.at[part(h, k), :], ch=mirror))
        shared.append(send(all_act.at[part(h, k), :], all_act.at[part(h, k), :], ch=partner))

    for copy in rest:
        copy.wait()
    for at in range(ns):
        proj_t[pl.ds(at * own, own), :] = proj_v[:, pl.ds(at * own, own)].T
    for copy in wide_own:
        copy.wait()
    for copy in wide:
        copy.wait_recv()
    table = table_v[...]
    spec = to_spectrum(wide_in[...], table)
    filt = (spec[0][:own], spec[1][:own])
    cot = (spec[0][own:], spec[1][own:])
    taps_own = taps_v[...]
    taps_high = taps_own.astype(jnp.bfloat16)
    taps_low = (taps_own - taps_high.astype(jnp.float32)).astype(jnp.bfloat16)
    table_top = table_v[pl.ds(0, taps_own.shape[1]), :]
    high = to_spectrum(taps_high, table_top)
    low = to_spectrum(taps_low, table_top)
    taps = (high[0] + low[0], high[1] + low[1])
    back = from_spectrum(*times_conj(cot, filt), table).astype(jnp.bfloat16).astype(jnp.float32)

    for k in range(pieces):
        crossed[k].wait_recv()
        shared.append(
            send(all_act.at[part(mirror, k), :], all_act.at[part(mirror, k), :], ch=partner)
        )
    for copy in shared:
        copy.wait_recv()

    def half_of(index, c):
        return pl.ds(pl.multiple_of(index * own + c * half, half), half)

    def sum_to(d, c):
        return send(
            part_sum.at[half_of((s + d) % ns, c), :],
            got_sum.at[d - 1, pl.ds(c * half, half), :],
            seq=(s + d) % ns,
        )

    reduced = [[], []]
    for d in range(1, ns):
        got = jnp.dot(
            proj_t[block((s + d) % ns, own), :],
            all_act[...],
            preferred_element_type=jnp.float32,
        )
        part_sum[block((s + d) % ns, own), :] = got.astype(jnp.bfloat16)
        reduced[0].append(sum_to(d, 0))
    for d in range(1, ns):
        reduced[1].append(sum_to(d, 1))
    mixed = jnp.dot(
        proj_t[block(s, own), :], all_act[...], preferred_element_type=jnp.float32
    )
    def place(p):
        return p % 2 * (ns // 2) + p // 2

    def stage_of(t, i):
        return block((t + 1 + i) % 2, length // 2)

    gathered, mediums, gates = ([], []), [], []
    for c in range(2):
        at = slice(c * half, (c + 1) * half)
        summed = mixed[at]
        for d in range(1, ns):
            reduced[c][d - 1].wait_recv()
            summed = summed + got_sum[d - 1, pl.ds(c * half, half), :].astype(jnp.float32)
        values = summed.astype(jnp.bfloat16)
        gate = jax.nn.sigmoid(values.astype(jnp.float32))
        grad_medium = (back[at] * gate).astype(jnp.bfloat16)
        spec = to_spectrum(jnp.concatenate([values, grad_medium], axis=0), table)
        taps_half = (taps[0][at], taps[1][at])
        both = stacked(
            times((spec[0][:half], spec[1][:half]), taps_half),
            times_conj((spec[0][half:], spec[1][half:]), taps_half),
        )
        both = from_spectrum(*both, table)
        medium, through = both[:half], both[half:]
        grads = (through + back[at] * medium * gate * (1.0 - gate)).astype(jnp.bfloat16)
        for p in range(ns):
            all_grad[half_of(s, c), pl.ds(place(p) * span, span)] = grads[
                :, p * span : (p + 1) * span
            ]
        for i in range(2):
            for d in range(1, ns):
                where = (half_of(s, c), stage_of((s + d) % ns, i))
                gathered[i].append(
                    send(all_grad.at[where], all_grad.at[where], seq=(s + d) % ns)
                )
        mediums.append(medium)
        gates.append(gate)
    medium, gate = jnp.concatenate(mediums, axis=0), jnp.concatenate(gates, axis=0)

    gated = (medium * gate).astype(jnp.bfloat16)
    conv = from_spectrum(*times(to_spectrum(gated, table), filt), table)
    conv_own[...] = conv.astype(jnp.bfloat16)
    returned = [
        send(
            conv_own.at[:, block((s + d) % ns, span)],
            conv_got.at[block(s, own), :],
            seq=(s + d) % ns,
        )
        for d in range(1, ns)
    ]
    conv_got[block(s, own), :] = conv_own[:, block(s, span)]

    def partial(to, i):
        return jnp.dot(
            proj_v[block(to, quarter), :],
            all_grad[:, stage_of(s, i)],
            preferred_element_type=jnp.float32,
        )

    seconds, mirrored = [], []
    for i in range(2):
        lanes = stage_of(s, i)
        for copy in gathered[i]:
            copy.wait_recv()
        pair = []
        for side, to in enumerate((across, partner)):
            part_grad[block(to, quarter), lanes] = partial(to, i).astype(jnp.bfloat16)
            pair.append(
                send(
                    part_grad.at[block(to, quarter), lanes],
                    pair_grad.at[side, :, lanes],
                    ch=partner,
                )
            )
        kept = partial(mirror, i)
        pair[0].wait_recv()
        kept = kept + pair_grad[0, :, lanes].astype(jnp.float32)
        mirror_send[:, lanes] = kept.astype(jnp.bfloat16)
        copies = []
        for k in range(pieces):
            at = pl.ds(k * piece, piece)
            copies.append(send(mirror_send.at[at, lanes], mirror_got.at[at, lanes], ch=mirror))
        seconds.append(pair[1])
        mirrored.append(copies)
    placed = [[] for _ in range(pieces)]
    for i in range(2):
        lanes = stage_of(s, i)
        kept = partial(h, i)
        seconds[i].wait_recv()
        for k in range(pieces):
            at = pl.ds(k * piece, piece)
            some = kept[k * piece : (k + 1) * piece] + pair_grad[1, at, lanes].astype(jnp.float32)
            mirrored[i][k].wait_recv()
            some = some + mirror_got[at, lanes].astype(jnp.float32)
            total_grad[at, lanes] = some.astype(jnp.bfloat16)
            for d in range(1, ns):
                if (d + 1 + i) % 2 == 0:
                    to = (s + d) % ns
                    placed[k].append(
                        send(
                            total_grad.at[at, block(place(to), span)],
                            turned.at[s, at, :],
                            seq=to,
                        )
                    )
            if i == 1:
                turned[s, at, :] = total_grad[at, block(place(s), span)]
    final = []
    for k in range(pieces):
        at = pl.ds(k * piece, piece)
        for copy in placed[k]:
            copy.wait_recv()
        final += [
            send(turned.at[(h + d) % nc, at, :], grad_got.at[part(h, k), :], ch=(h + d) % nc)
            for d in range(1, nc)
        ]
        grad_got[part(h, k), :] = turned[h, at, :]
    for copy in returned:
        copy.wait_recv()
    conv_ref[...] = conv_got[...]
    for copy in final:
        copy.wait_recv()
    grad_ref[...] = grad_got[...]
    for copy in started:
        copy.wait_send()


def fused_on_device(ns, nc, activations, projection, medium_taps, long_filters, cotangent):
    rows, span = activations.shape
    channels = long_filters.shape[0]
    own = channels // ns
    taps = medium_taps.shape[1]
    length = span * ns
    quarter = rows // nc
    pieces = 2
    copies = 9 * pieces + 3 * pieces + 3 * pieces + 6 * pieces + 24 + 16
    vmem = pl.BlockSpec(memory_space=pltpu.VMEM)
    hbm = pl.BlockSpec(memory_space=pltpu.HBM)
    bf16 = jnp.bfloat16
    return pl.pallas_call(
        functools.partial(fused_kernel, ns, nc, pieces),
        out_shape=(
            jax.ShapeDtypeStruct((channels, span), bf16),
            jax.ShapeDtypeStruct((rows, span), bf16),
        ),
        in_specs=[hbm] * 6,
        out_specs=(vmem, vmem),
        scratch_shapes=[
            pltpu.VMEM((nc, quarter, span), bf16),
            pltpu.VMEM((rows, length), bf16),
            pltpu.VMEM((2 * own, length), bf16),
            pltpu.VMEM((channels, length), bf16),
            pltpu.VMEM((ns - 1, own, length), bf16),
            pltpu.VMEM((own, length), bf16),
            pltpu.VMEM((channels, span), bf16),
            pltpu.VMEM((channels, length), bf16),
            pltpu.VMEM((rows, length), bf16),
            pltpu.VMEM((2, quarter, length), bf16),
            pltpu.VMEM((quarter, length), bf16),
            pltpu.VMEM((quarter, length), bf16),
            pltpu.VMEM((quarter, length), bf16),
            pltpu.VMEM((ns, quarter, span), bf16),
            pltpu.VMEM((rows, span), bf16),
            pltpu.VMEM((rows, channels), bf16),
            pltpu.VMEM((channels, rows), bf16),
            pltpu.VMEM((own, taps), jnp.float32),
            pltpu.VMEM((length, 2 * length), bf16),
            pltpu.SemaphoreType.DMA((copies,)),
            pltpu.SemaphoreType.DMA((copies,)),
            pltpu.SemaphoreType.DMA((8,)),
        ],
        compiler_params=pltpu.CompilerParams(
            collective_id=0, has_side_effects=True, vmem_limit_bytes=60 * 1024 * 1024
        ),
    )(activations, projection, medium_taps, long_filters, cotangent, transform_table(length))


def solution(mesh):
    ns, nc = mesh.shape["seq"], mesh.shape["ch"]

    def on_any(activations, projection, medium_taps, long_filters, cotangent):
        arrays = (activations, projection, medium_taps, long_filters, cotangent)
        table_bytes = 4 * (activations.shape[1] * ns) ** 2
        if ns == nc == 4 and table_bytes <= 4 << 20:
            return fused_on_device(ns, nc, *arrays)
        return on_device(*arrays)

    return jax.shard_map(
        on_any,
        mesh=mesh,
        in_specs=(
            P("ch", ("grp", "seq")),
            P("seq", "ch"),
            P("ch", None),
            P("ch", "seq"),
            P("ch", ("grp", "seq")),
        ),
        out_specs=(P("ch", ("grp", "seq")), P("ch", ("grp", "seq"))),
        check_vma=False,
    )
```

```python
import functools
import math

import jax
import jax.numpy as jnp
import numpy as np
from jax import lax
from jax.experimental import pallas as pl
from jax.experimental.pallas import tpu as pltpu
from jax.sharding import PartitionSpec as P

exact_mode = lax.Precision.HIGH


def medium_forward(padded, tap_weights, length):
    tap_count = tap_weights.shape[1]
    summed = jnp.zeros((padded.shape[0], length), jnp.float32)
    for offset in range(tap_count):
        begin_col = tap_count - 1 - offset
        summed = (
            summed + tap_weights[:, offset : offset + 1] * padded[:, begin_col : begin_col + length]
        )
    return summed


def medium_backward(padded, tap_weights, length):
    tap_count = tap_weights.shape[1]
    summed = jnp.zeros((padded.shape[0], length), jnp.float32)
    for offset in range(tap_count):
        summed = summed + tap_weights[:, offset : offset + 1] * padded[:, offset : offset + length]
    return summed


def dft_tables(length):
    points = 2 * length
    columns = 128
    row_count = points // columns
    half_rows = row_count // 2
    freq_rows = jnp.arange(row_count, dtype=jnp.int32)
    time_rows = jnp.arange(half_rows, dtype=jnp.int32)
    lane_index = jnp.arange(columns, dtype=jnp.int32)
    angle_first = (
        2.0
        * math.pi
        / row_count
        * (freq_rows[:, None] * time_rows[None, :] % row_count).astype(jnp.float32)
    )
    angle_twist = (
        2.0
        * math.pi
        / points
        * (freq_rows[:, None] * lane_index[None, :] % points).astype(jnp.float32)
    )
    angle_last = (
        2.0
        * math.pi
        / columns
        * (lane_index[:, None] * lane_index[None, :] % columns).astype(jnp.float32)
    )
    return (
        jnp.cos(angle_first),
        jnp.sin(angle_first),
        jnp.cos(angle_twist),
        jnp.sin(angle_twist),
        jnp.cos(angle_last),
        jnp.sin(angle_last),
    )


def forward_dft(signal, tables):
    cos_first, sin_first, cos_twist, sin_twist, cos_last, sin_last = tables
    channels = signal.shape[0]
    shaped = signal.reshape(channels, cos_first.shape[1], 128)
    section_re = jnp.einsum("kn,cnq->ckq", cos_first, shaped, precision=exact_mode)
    section_im = -jnp.einsum("kn,cnq->ckq", sin_first, shaped, precision=exact_mode)
    twist_re = section_re * cos_twist + section_im * sin_twist
    twist_im = section_im * cos_twist - section_re * sin_twist
    spec_re = jnp.einsum("ckq,qm->ckm", twist_re, cos_last, precision=exact_mode) + jnp.einsum(
        "ckq,qm->ckm", twist_im, sin_last, precision=exact_mode
    )
    spec_im = jnp.einsum("ckq,qm->ckm", twist_im, cos_last, precision=exact_mode) - jnp.einsum(
        "ckq,qm->ckm", twist_re, sin_last, precision=exact_mode
    )
    return (spec_re, spec_im)


def inverse_dft(spec_re, spec_im, tables):
    cos_first, sin_first, cos_twist, sin_twist, cos_last, sin_last = tables
    channels = spec_re.shape[0]
    half_rows = cos_first.shape[1]
    inner_re = jnp.einsum("ckq,qm->ckm", spec_re, cos_last, precision=exact_mode) - jnp.einsum(
        "ckq,qm->ckm", spec_im, sin_last, precision=exact_mode
    )
    inner_im = jnp.einsum("ckq,qm->ckm", spec_im, cos_last, precision=exact_mode) + jnp.einsum(
        "ckq,qm->ckm", spec_re, sin_last, precision=exact_mode
    )
    turned_re = inner_re * cos_twist - inner_im * sin_twist
    turned_im = inner_im * cos_twist + inner_re * sin_twist
    output = jnp.einsum("kn,ckq->cnq", cos_first, turned_re, precision=exact_mode) - jnp.einsum(
        "kn,ckq->cnq", sin_first, turned_im, precision=exact_mode
    )
    points = 2 * half_rows * 128
    return (output / points).reshape(channels, half_rows * 128)


def causal_apply(signal, filt_re, filt_im, tables, conjugate):
    sig_re, sig_im = forward_dft(signal, tables)
    if conjugate:
        prod_re = sig_re * filt_re + sig_im * filt_im
        prod_im = sig_im * filt_re - sig_re * filt_im
    else:
        prod_re = sig_re * filt_re - sig_im * filt_im
        prod_im = sig_im * filt_re + sig_re * filt_im
    return inverse_dft(prod_re, prod_im, tables)


def on_device(activations, projection, medium_taps, long_filters, cotangent):
    tap_count = medium_taps.shape[1]
    whole_in = lax.all_gather(activations, "ch", axis=0, tiled=True)
    mixed_sum = lax.dot_general(
        lax.all_gather(projection, "seq", axis=0, tiled=True),
        whole_in,
        (((0,), (0,)), ((), ())),
        preferred_element_type=jnp.float32,
    )
    values = mixed_sum.astype(jnp.bfloat16)
    channel_count = values.shape[0] // lax.axis_size("seq")
    own_taps = lax.dynamic_slice_in_dim(
        medium_taps, lax.axis_index("seq") * channel_count, channel_count, 0
    )
    arrived, filters_ch = (
        lax.all_to_all(values, "seq", split_axis=0, concat_axis=1, tiled=True),
        lax.all_to_all(long_filters, "seq", split_axis=0, concat_axis=1, tiled=True),
    )
    tables = dft_tables(arrived.shape[1])
    filt_re, filt_im = forward_dft(filters_ch.astype(jnp.float32), tables)
    values_ch = arrived.astype(jnp.float32)
    padded_ch = jnp.pad(values_ch, ((0, 0), (tap_count - 1, 0)))
    conv_ch = medium_forward(padded_ch, own_taps, arrived.shape[1])
    gate_ch = jax.nn.sigmoid(values_ch)
    signal = lax.optimization_barrier((conv_ch * gate_ch).astype(jnp.bfloat16)).astype(jnp.float32)
    kept_state = (conv_ch, gate_ch)
    output_ch = causal_apply(signal, filt_re, filt_im, tables, False).astype(jnp.bfloat16)
    output_ch, context = (output_ch, (filt_re, filt_im, tables, kept_state))
    conv_out = lax.all_to_all(output_ch, "seq", split_axis=1, concat_axis=0, tiled=True)
    grad_ch = lax.all_to_all(cotangent, "seq", split_axis=0, concat_axis=1, tiled=True)
    filt_re, filt_im, tables, kept_state = context
    back_grad = lax.optimization_barrier(
        causal_apply(grad_ch.astype(jnp.float32), filt_re, filt_im, tables, True).astype(
            jnp.bfloat16
        )
    )
    conv_ch, gate_ch = kept_state
    grad_wide = back_grad.astype(jnp.float32)
    conv_grad = lax.optimization_barrier((grad_wide * gate_ch).astype(jnp.bfloat16)).astype(
        jnp.float32
    )
    padded_grad = jnp.pad(conv_grad, ((0, 0), (0, tap_count - 1)))
    through = medium_backward(padded_grad, own_taps, conv_grad.shape[1])
    gate_grad = grad_wide * conv_ch * gate_ch * (1.0 - gate_ch)
    back_ch = (through + gate_grad).astype(jnp.bfloat16)
    returned = lax.all_to_all(back_ch, "seq", split_axis=1, concat_axis=0, tiled=True)
    partial_grad = jnp.dot(
        lax.all_gather(projection, "seq", axis=0, tiled=True),
        returned,
        preferred_element_type=jnp.float32,
    )
    input_grad = lax.psum_scatter(
        partial_grad.astype(jnp.bfloat16), "ch", scatter_dimension=0, tiled=True
    )
    return (conv_out, input_grad)


MESH = pl.DeviceIdType.MESH


def transform_table(length):
    points = 2 * length
    turns = np.arange(length)[:, None] * (2 * np.arange(length)[None, :] + 1) % (2 * points)
    angles = turns * (math.pi / points)
    return jnp.asarray(np.concatenate([np.cos(angles), np.sin(angles)], axis=1), jnp.bfloat16)


def to_spectrum(signal, table):
    spectrum = jnp.dot(signal, table, preferred_element_type=jnp.float32)
    half = spectrum.shape[1] // 2
    return spectrum[:, :half], spectrum[:, half:]


def from_spectrum(even, odd, table):
    both = jnp.concatenate([even, odd], axis=1).astype(jnp.bfloat16)
    signal = lax.dot_general(
        both, table, (((1,), (1,)), ((), ())), preferred_element_type=jnp.float32
    )
    return signal * (1.0 / table.shape[0])


def times(left, right):
    return left[0] * right[0] - left[1] * right[1], left[0] * right[1] + left[1] * right[0]


def times_conj(left, right):
    return left[0] * right[0] + left[1] * right[1], left[1] * right[0] - left[0] * right[1]


def stacked(first, second):
    return (
        jnp.concatenate([first[0], second[0]], axis=0),
        jnp.concatenate([first[1], second[1]], axis=0),
    )


def fused_kernel(
    ns,
    nc,
    pieces,
    act_ref,
    proj_ref,
    taps_ref,
    filt_ref,
    cot_ref,
    table_ref,
    conv_ref,
    grad_ref,
    held_act,
    all_act,
    wide_in,
    part_sum,
    got_sum,
    far_got,
    conv_own,
    conv_got,
    all_grad,
    part_grad,
    pair_grad,
    mirror_send,
    mirror_got,
    total_grad,
    turned,
    grad_got,
    proj_v,
    proj_t,
    taps_v,
    table_v,
    send_sems,
    recv_sems,
    load_sems,
):
    s = lax.axis_index("seq")
    h = lax.axis_index("ch")
    rows = act_ref.shape[0]
    span = act_ref.shape[1]
    own = filt_ref.shape[0] // ns
    quarter = rows // nc
    piece = quarter // pieces
    length = span * ns
    partner = h + 1 - 2 * (h % 2)
    mirror = (h + nc // 2) % nc
    across = (partner + nc // 2) % nc
    started, loads = [], []

    @pl.when(s == 0)
    def _():
        got_sum[0] = jnp.zeros_like(got_sum[0])

    @pl.when(s == ns - 1)
    def _():
        got_sum[ns - 2] = jnp.zeros_like(got_sum[ns - 2])

    half = own // 2

    def block(index, size):
        return pl.ds(pl.multiple_of(index * size, size), size)

    def part(index, k):
        return pl.ds(pl.multiple_of(index * quarter + k * piece, piece), piece)

    def send(src, dst, when=None, into=None, **where):
        slot = len(started)
        into = slot if into is None else into
        copy = pltpu.make_async_remote_copy(
            src_ref=src,
            dst_ref=dst,
            send_sem=send_sems.at[slot],
            recv_sem=recv_sems.at[into],
            device_id=where,
            device_id_type=MESH,
        )
        if when is None:
            copy.start()
        else:
            pl.when(when)(lambda: copy.start())
        started.append((copy, when))
        return copy

    def load(src, dst):
        copy = pltpu.make_async_copy(src, dst, load_sems.at[len(loads)])
        copy.start()
        loads.append(copy)
        return copy

    barrier = pltpu.get_barrier_semaphore()
    for d in range(1, ns):
        pl.semaphore_signal(
            barrier, inc=1, device_id={"seq": (s + d) % ns}, device_id_type=MESH
        )
    for d in range(1, nc):
        pl.semaphore_signal(barrier, inc=1, device_id={"ch": (h + d) % nc}, device_id_type=MESH)
    act_own = load(act_ref.at[block(h, quarter), :], held_act.at[h])
    wide_own = [
        load(ref.at[block(s, own), :], wide_in.at[pl.ds(at * own, own), block(s, span)])
        for at, ref in enumerate((filt_ref, cot_ref))
    ]
    rest = [
        load(table_ref, table_v),
        load(taps_ref.at[block(s, own), :], taps_v),
        load(proj_ref, proj_v),
    ]
    pl.semaphore_wait(barrier, ns + nc - 2)

    spread = []
    for k in range(pieces):
        spread.append(
            [
                send(
                    act_ref.at[part((h + d) % nc, k), :],
                    held_act.at[h, pl.ds(k * piece, piece), :],
                    ch=(h + d) % nc,
                )
                for d in range(1, nc)
            ]
        )
    act_own.wait()
    moved = []
    for k in range(pieces):
        for copy in spread[k]:
            copy.wait_recv()
        moved.append(
            [
                send(
                    held_act.at[(s + d) % ns, pl.ds(k * piece, piece), :],
                    all_act.at[part(h, k), block(s, span)],
                    seq=(s + d) % ns,
                )
                for d in range(1, ns)
            ]
        )
    all_act[block(h, quarter), block(s, span)] = held_act[s]
    wide = []
    for at, ref in enumerate((filt_ref, cot_ref)):
        for d in range(1, ns):
            wide.append(
                send(
                    ref.at[block((s + d) % ns, own), :],
                    wide_in.at[pl.ds(at * own, own), block(s, span)],
                    seq=(s + d) % ns,
                )
            )
    shared, crossed = [], []
    for k in range(pieces):
        for copy in moved[k]:
            copy.wait_recv()
        crossed.append(send(all_act.at[part(h, k), :], all_act.at[part(h, k), :], ch=mirror))
        shared.append(send(all_act.at[part(h, k), :], all_act.at[part(h, k), :], ch=partner))

    for copy in rest:
        copy.wait()
    for at in range(ns):
        proj_t[pl.ds(at * own, own), :] = proj_v[:, pl.ds(at * own, own)].T
    for copy in wide_own:
        copy.wait()
    for copy in wide:
        copy.wait_recv()
    table = table_v[...]
    spec = to_spectrum(wide_in[...], table)
    filt = (spec[0][:own], spec[1][:own])
    cot = (spec[0][own:], spec[1][own:])
    taps_own = taps_v[...]
    taps_high = taps_own.astype(jnp.bfloat16)
    taps_low = (taps_own - taps_high.astype(jnp.float32)).astype(jnp.bfloat16)
    table_top = table_v[pl.ds(0, taps_own.shape[1]), :]
    high = to_spectrum(taps_high, table_top)
    low = to_spectrum(taps_low, table_top)
    taps = (high[0] + low[0], high[1] + low[1])
    back = from_spectrum(*times_conj(cot, filt), table).astype(jnp.bfloat16).astype(jnp.float32)

    for k in range(pieces):
        crossed[k].wait_recv()
        shared.append(
            send(all_act.at[part(mirror, k), :], all_act.at[part(mirror, k), :], ch=partner)
        )
    for copy in shared:
        copy.wait_recv()

    def half_of(index, c):
        return pl.ds(pl.multiple_of(index * own + c * half, half), half)

    inner = (s != 0) & (s != ns - 1)
    near = {1: s != ns - 1, 2: (s == 0) | (s == ns - 1), 3: s != 0}
    reduced, sum_slots, far = {}, {}, {}

    def sum_to(d, c):
        rows_to = half_of((s + d) % ns, c)
        at = pl.ds(c * half, half)
        if d != 2:
            far[c] = send(
                part_sum.at[rows_to, :],
                far_got.at[at, :],
                when=s == (ns - 1 if d == 1 else 0),
                into=sum_slots.setdefault(("far", c), len(started)),
                seq=ns - 2 if d == 1 else 1,
            )
        sum_slots[c, d] = len(started)
        reduced[c, d] = send(
            part_sum.at[rows_to, :],
            got_sum.at[d - 1, at, :],
            when=near[d],
            seq=(s + d) % ns,
        )

    for d in (3, 1, 2):
        got = jnp.dot(
            proj_t[block((s + d) % ns, own), :],
            all_act[...],
            preferred_element_type=jnp.float32,
        )
        part_sum[block((s + d) % ns, own), :] = got.astype(jnp.bfloat16)
        sum_to(d, 0)
    for d in (3, 1, 2):
        sum_to(d, 1)
    mixed = jnp.dot(
        proj_t[block(s, own), :], all_act[...], preferred_element_type=jnp.float32
    )
    for c in range(2):
        at = pl.ds(c * half, half)
        rows_to = half_of((s + 2) % ns, c)

        @pl.when(inner)
        def _(c=c, at=at, rows_to=rows_to):
            far[c].wait_recv()
            joined = part_sum[rows_to, :].astype(jnp.float32) + far_got[at, :].astype(jnp.float32)
            part_sum[rows_to, :] = joined.astype(jnp.bfloat16)

        send(
            part_sum.at[rows_to, :],
            got_sum.at[1, at, :],
            when=inner,
            into=sum_slots[c, 2],
            seq=(s + 2) % ns,
        )

    def place(p):
        return p % 2 * (ns // 2) + p // 2

    def stage_of(t, i):
        return block((t + 1 + i) % 2, length // 2)

    def relay(c):
        for i in range(2):
            gathered[c, i, 2].wait_recv()
            where = (half_of((s + 2) % ns, c), stage_of(s, i))
            for end, d in ((0, 1), (ns - 1, 3)):
                send(
                    all_grad.at[where],
                    all_grad.at[where],
                    when=s == (1 if end == 0 else ns - 2),
                    into=slots[c, 1 - i, d],
                    seq=end,
                )

    gathered, slots, mediums, gates = {}, {}, [], []
    for c in range(2):
        at = slice(c * half, (c + 1) * half)
        summed = mixed[at]
        for d in range(1, ns):
            if d == 2:
                reduced[c, d].wait_recv()
            else:
                pl.when(s != (0 if d == 1 else ns - 1))(reduced[c, d].wait_recv)
            summed = summed + got_sum[d - 1, pl.ds(c * half, half), :].astype(jnp.float32)
        values = summed.astype(jnp.bfloat16)
        gate = jax.nn.sigmoid(values.astype(jnp.float32))
        grad_medium = (back[at] * gate).astype(jnp.bfloat16)
        spec = to_spectrum(jnp.concatenate([values, grad_medium], axis=0), table)
        taps_half = (taps[0][at], taps[1][at])
        both = stacked(
            times((spec[0][:half], spec[1][:half]), taps_half),
            times_conj((spec[0][half:], spec[1][half:]), taps_half),
        )
        both = from_spectrum(*both, table)
        medium, through = both[:half], both[half:]
        grads = (through + back[at] * medium * gate * (1.0 - gate)).astype(jnp.bfloat16)
        for p in range(ns):
            all_grad[half_of(s, c), pl.ds(place(p) * span, span)] = grads[
                :, p * span : (p + 1) * span
            ]
        for i, d in [(0, 2), (1, 2), (0, 1), (0, 3), (1, 1), (1, 3)]:
            where = (half_of(s, c), stage_of((s + d) % ns, i))
            near = {1: s != ns - 1, 2: None, 3: s != 0}[d]
            slots[c, i, d] = len(started)
            gathered[c, i, d] = send(
                all_grad.at[where], all_grad.at[where], when=near, seq=(s + d) % ns
            )
        mediums.append(medium)
        gates.append(gate)
    medium, gate = jnp.concatenate(mediums, axis=0), jnp.concatenate(gates, axis=0)

    relay(0)
    gated = (medium * gate).astype(jnp.bfloat16)
    conv = from_spectrum(*times(to_spectrum(gated, table), filt), table)
    conv_own[...] = conv.astype(jnp.bfloat16)
    returned = [
        send(
            conv_own.at[:, block((s + d) % ns, span)],
            conv_got.at[block(s, own), :],
            seq=(s + d) % ns,
        )
        for d in range(1, ns)
    ]
    conv_got[block(s, own), :] = conv_own[:, block(s, span)]

    relay(1)
    def partial(to, i):
        return jnp.dot(
            proj_v[block(to, quarter), :],
            all_grad[:, stage_of(s, i)],
            preferred_element_type=jnp.float32,
        )

    seconds, mirrored = [], []
    for i in range(2):
        lanes = stage_of(s, i)
        for c, d in ((0, 1), (0, 3), (1, 1), (1, 3)):
            gathered[c, i, d].wait_recv()
        pair = []
        for side, to in enumerate((across, partner)):
            part_grad[block(to, quarter), lanes] = partial(to, i).astype(jnp.bfloat16)
            pair.append(
                send(
                    part_grad.at[block(to, quarter), lanes],
                    pair_grad.at[side, :, lanes],
                    ch=partner,
                )
            )
        kept = partial(mirror, i)
        pair[0].wait_recv()
        kept = kept + pair_grad[0, :, lanes].astype(jnp.float32)
        mirror_send[:, lanes] = kept.astype(jnp.bfloat16)
        copies = []
        for k in range(pieces):
            at = pl.ds(k * piece, piece)
            copies.append(send(mirror_send.at[at, lanes], mirror_got.at[at, lanes], ch=mirror))
        seconds.append(pair[1])
        mirrored.append(copies)
    placed = [[] for _ in range(pieces)]
    for i in range(2):
        lanes = stage_of(s, i)
        kept = partial(h, i)
        seconds[i].wait_recv()
        for k in range(pieces):
            at = pl.ds(k * piece, piece)
            some = kept[k * piece : (k + 1) * piece] + pair_grad[1, at, lanes].astype(jnp.float32)
            mirrored[i][k].wait_recv()
            some = some + mirror_got[at, lanes].astype(jnp.float32)
            total_grad[at, lanes] = some.astype(jnp.bfloat16)
            for d in range(1, ns):
                if (d + 1 + i) % 2 == 0:
                    to = (s + d) % ns
                    placed[k].append(
                        send(
                            total_grad.at[at, block(place(to), span)],
                            turned.at[s, at, :],
                            seq=to,
                        )
                    )
            if i == 1:
                turned[s, at, :] = total_grad[at, block(place(s), span)]
    final = []
    for k in range(pieces):
        at = pl.ds(k * piece, piece)
        for copy in placed[k]:
            copy.wait_recv()
        final += [
            send(turned.at[(h + d) % nc, at, :], grad_got.at[part(h, k), :], ch=(h + d) % nc)
            for d in range(1, nc)
        ]
        grad_got[part(h, k), :] = turned[h, at, :]
    for copy in returned:
        copy.wait_recv()
    conv_ref[...] = conv_got[...]
    for copy in final:
        copy.wait_recv()
    grad_ref[...] = grad_got[...]
    for copy, when in started:
        if when is None:
            copy.wait_send()
        else:
            pl.when(when)(lambda copy=copy: copy.wait_send())


def fused_on_device(ns, nc, activations, projection, medium_taps, long_filters, cotangent):
    rows, span = activations.shape
    channels = long_filters.shape[0]
    own = channels // ns
    taps = medium_taps.shape[1]
    length = span * ns
    quarter = rows // nc
    pieces = 2
    copies = 9 * pieces + 3 * pieces + 3 * pieces + 6 * pieces + 24 + 40
    vmem = pl.BlockSpec(memory_space=pltpu.VMEM)
    hbm = pl.BlockSpec(memory_space=pltpu.HBM)
    bf16 = jnp.bfloat16
    return pl.pallas_call(
        functools.partial(fused_kernel, ns, nc, pieces),
        out_shape=(
            jax.ShapeDtypeStruct((channels, span), bf16),
            jax.ShapeDtypeStruct((rows, span), bf16),
        ),
        in_specs=[hbm] * 6,
        out_specs=(vmem, vmem),
        scratch_shapes=[
            pltpu.VMEM((nc, quarter, span), bf16),
            pltpu.VMEM((rows, length), bf16),
            pltpu.VMEM((2 * own, length), bf16),
            pltpu.VMEM((channels, length), bf16),
            pltpu.VMEM((ns - 1, own, length), bf16),
            pltpu.VMEM((own, length), bf16),
            pltpu.VMEM((own, length), bf16),
            pltpu.VMEM((channels, span), bf16),
            pltpu.VMEM((channels, length), bf16),
            pltpu.VMEM((rows, length), bf16),
            pltpu.VMEM((2, quarter, length), bf16),
            pltpu.VMEM((quarter, length), bf16),
            pltpu.VMEM((quarter, length), bf16),
            pltpu.VMEM((quarter, length), bf16),
            pltpu.VMEM((ns, quarter, span), bf16),
            pltpu.VMEM((rows, span), bf16),
            pltpu.VMEM((rows, channels), bf16),
            pltpu.VMEM((channels, rows), bf16),
            pltpu.VMEM((own, taps), jnp.float32),
            pltpu.VMEM((length, 2 * length), bf16),
            pltpu.SemaphoreType.DMA((copies,)),
            pltpu.SemaphoreType.DMA((copies,)),
            pltpu.SemaphoreType.DMA((8,)),
        ],
        compiler_params=pltpu.CompilerParams(
            collective_id=0, has_side_effects=True, vmem_limit_bytes=60 * 1024 * 1024
        ),
    )(activations, projection, medium_taps, long_filters, cotangent, transform_table(length))


def solution(mesh):
    ns, nc = mesh.shape["seq"], mesh.shape["ch"]

    def on_any(activations, projection, medium_taps, long_filters, cotangent):
        arrays = (activations, projection, medium_taps, long_filters, cotangent)
        table_bytes = 4 * (activations.shape[1] * ns) ** 2
        if ns == nc == 4 and table_bytes <= 4 << 20:
            return fused_on_device(ns, nc, *arrays)
        return on_device(*arrays)

    return jax.shard_map(
        on_any,
        mesh=mesh,
        in_specs=(
            P("ch", ("grp", "seq")),
            P("seq", "ch"),
            P("ch", None),
            P("ch", "seq"),
            P("ch", ("grp", "seq")),
        ),
        out_specs=(P("ch", ("grp", "seq")), P("ch", ("grp", "seq"))),
        check_vma=False,
    )
```

```python
import functools
import math

import jax
import jax.numpy as jnp
import numpy as np
from jax import lax
from jax.experimental import pallas as pl
from jax.experimental.pallas import tpu as pltpu
from jax.sharding import PartitionSpec as P

exact_mode = lax.Precision.HIGH


def medium_forward(padded, tap_weights, length):
    tap_count = tap_weights.shape[1]
    summed = jnp.zeros((padded.shape[0], length), jnp.float32)
    for offset in range(tap_count):
        begin_col = tap_count - 1 - offset
        summed = (
            summed + tap_weights[:, offset : offset + 1] * padded[:, begin_col : begin_col + length]
        )
    return summed


def medium_backward(padded, tap_weights, length):
    tap_count = tap_weights.shape[1]
    summed = jnp.zeros((padded.shape[0], length), jnp.float32)
    for offset in range(tap_count):
        summed = summed + tap_weights[:, offset : offset + 1] * padded[:, offset : offset + length]
    return summed


def dft_tables(length):
    points = 2 * length
    columns = 128
    row_count = points // columns
    half_rows = row_count // 2
    freq_rows = jnp.arange(row_count, dtype=jnp.int32)
    time_rows = jnp.arange(half_rows, dtype=jnp.int32)
    lane_index = jnp.arange(columns, dtype=jnp.int32)
    angle_first = (
        2.0
        * math.pi
        / row_count
        * (freq_rows[:, None] * time_rows[None, :] % row_count).astype(jnp.float32)
    )
    angle_twist = (
        2.0
        * math.pi
        / points
        * (freq_rows[:, None] * lane_index[None, :] % points).astype(jnp.float32)
    )
    angle_last = (
        2.0
        * math.pi
        / columns
        * (lane_index[:, None] * lane_index[None, :] % columns).astype(jnp.float32)
    )
    return (
        jnp.cos(angle_first),
        jnp.sin(angle_first),
        jnp.cos(angle_twist),
        jnp.sin(angle_twist),
        jnp.cos(angle_last),
        jnp.sin(angle_last),
    )


def forward_dft(signal, tables):
    cos_first, sin_first, cos_twist, sin_twist, cos_last, sin_last = tables
    channels = signal.shape[0]
    shaped = signal.reshape(channels, cos_first.shape[1], 128)
    section_re = jnp.einsum("kn,cnq->ckq", cos_first, shaped, precision=exact_mode)
    section_im = -jnp.einsum("kn,cnq->ckq", sin_first, shaped, precision=exact_mode)
    twist_re = section_re * cos_twist + section_im * sin_twist
    twist_im = section_im * cos_twist - section_re * sin_twist
    spec_re = jnp.einsum("ckq,qm->ckm", twist_re, cos_last, precision=exact_mode) + jnp.einsum(
        "ckq,qm->ckm", twist_im, sin_last, precision=exact_mode
    )
    spec_im = jnp.einsum("ckq,qm->ckm", twist_im, cos_last, precision=exact_mode) - jnp.einsum(
        "ckq,qm->ckm", twist_re, sin_last, precision=exact_mode
    )
    return (spec_re, spec_im)


def inverse_dft(spec_re, spec_im, tables):
    cos_first, sin_first, cos_twist, sin_twist, cos_last, sin_last = tables
    channels = spec_re.shape[0]
    half_rows = cos_first.shape[1]
    inner_re = jnp.einsum("ckq,qm->ckm", spec_re, cos_last, precision=exact_mode) - jnp.einsum(
        "ckq,qm->ckm", spec_im, sin_last, precision=exact_mode
    )
    inner_im = jnp.einsum("ckq,qm->ckm", spec_im, cos_last, precision=exact_mode) + jnp.einsum(
        "ckq,qm->ckm", spec_re, sin_last, precision=exact_mode
    )
    turned_re = inner_re * cos_twist - inner_im * sin_twist
    turned_im = inner_im * cos_twist + inner_re * sin_twist
    output = jnp.einsum("kn,ckq->cnq", cos_first, turned_re, precision=exact_mode) - jnp.einsum(
        "kn,ckq->cnq", sin_first, turned_im, precision=exact_mode
    )
    points = 2 * half_rows * 128
    return (output / points).reshape(channels, half_rows * 128)


def causal_apply(signal, filt_re, filt_im, tables, conjugate):
    sig_re, sig_im = forward_dft(signal, tables)
    if conjugate:
        prod_re = sig_re * filt_re + sig_im * filt_im
        prod_im = sig_im * filt_re - sig_re * filt_im
    else:
        prod_re = sig_re * filt_re - sig_im * filt_im
        prod_im = sig_im * filt_re + sig_re * filt_im
    return inverse_dft(prod_re, prod_im, tables)


def on_device(activations, projection, medium_taps, long_filters, cotangent):
    tap_count = medium_taps.shape[1]
    whole_in = lax.all_gather(activations, "ch", axis=0, tiled=True)
    mixed_sum = lax.dot_general(
        lax.all_gather(projection, "seq", axis=0, tiled=True),
        whole_in,
        (((0,), (0,)), ((), ())),
        preferred_element_type=jnp.float32,
    )
    values = mixed_sum.astype(jnp.bfloat16)
    channel_count = values.shape[0] // lax.axis_size("seq")
    own_taps = lax.dynamic_slice_in_dim(
        medium_taps, lax.axis_index("seq") * channel_count, channel_count, 0
    )
    arrived, filters_ch = (
        lax.all_to_all(values, "seq", split_axis=0, concat_axis=1, tiled=True),
        lax.all_to_all(long_filters, "seq", split_axis=0, concat_axis=1, tiled=True),
    )
    tables = dft_tables(arrived.shape[1])
    filt_re, filt_im = forward_dft(filters_ch.astype(jnp.float32), tables)
    values_ch = arrived.astype(jnp.float32)
    padded_ch = jnp.pad(values_ch, ((0, 0), (tap_count - 1, 0)))
    conv_ch = medium_forward(padded_ch, own_taps, arrived.shape[1])
    gate_ch = jax.nn.sigmoid(values_ch)
    signal = lax.optimization_barrier((conv_ch * gate_ch).astype(jnp.bfloat16)).astype(jnp.float32)
    kept_state = (conv_ch, gate_ch)
    output_ch = causal_apply(signal, filt_re, filt_im, tables, False).astype(jnp.bfloat16)
    output_ch, context = (output_ch, (filt_re, filt_im, tables, kept_state))
    conv_out = lax.all_to_all(output_ch, "seq", split_axis=1, concat_axis=0, tiled=True)
    grad_ch = lax.all_to_all(cotangent, "seq", split_axis=0, concat_axis=1, tiled=True)
    filt_re, filt_im, tables, kept_state = context
    back_grad = lax.optimization_barrier(
        causal_apply(grad_ch.astype(jnp.float32), filt_re, filt_im, tables, True).astype(
            jnp.bfloat16
        )
    )
    conv_ch, gate_ch = kept_state
    grad_wide = back_grad.astype(jnp.float32)
    conv_grad = lax.optimization_barrier((grad_wide * gate_ch).astype(jnp.bfloat16)).astype(
        jnp.float32
    )
    padded_grad = jnp.pad(conv_grad, ((0, 0), (0, tap_count - 1)))
    through = medium_backward(padded_grad, own_taps, conv_grad.shape[1])
    gate_grad = grad_wide * conv_ch * gate_ch * (1.0 - gate_ch)
    back_ch = (through + gate_grad).astype(jnp.bfloat16)
    returned = lax.all_to_all(back_ch, "seq", split_axis=1, concat_axis=0, tiled=True)
    partial_grad = jnp.dot(
        lax.all_gather(projection, "seq", axis=0, tiled=True),
        returned,
        preferred_element_type=jnp.float32,
    )
    input_grad = lax.psum_scatter(
        partial_grad.astype(jnp.bfloat16), "ch", scatter_dimension=0, tiled=True
    )
    return (conv_out, input_grad)


MESH = pl.DeviceIdType.MESH


def transform_table(length):
    points = 2 * length
    turns = np.arange(length)[:, None] * (2 * np.arange(length)[None, :] + 1) % (2 * points)
    angles = turns * (math.pi / points)
    return jnp.asarray(np.concatenate([np.cos(angles), np.sin(angles)], axis=1), jnp.bfloat16)


def to_spectrum(signal, table):
    spectrum = jnp.dot(signal, table, preferred_element_type=jnp.float32)
    half = spectrum.shape[1] // 2
    return spectrum[:, :half], spectrum[:, half:]


def from_spectrum(even, odd, table):
    both = jnp.concatenate([even, odd], axis=1).astype(jnp.bfloat16)
    signal = lax.dot_general(
        both, table, (((1,), (1,)), ((), ())), preferred_element_type=jnp.float32
    )
    return signal * (1.0 / table.shape[0])


def times(left, right):
    return left[0] * right[0] - left[1] * right[1], left[0] * right[1] + left[1] * right[0]


def times_conj(left, right):
    return left[0] * right[0] + left[1] * right[1], left[1] * right[0] - left[0] * right[1]


def stacked(first, second):
    return (
        jnp.concatenate([first[0], second[0]], axis=0),
        jnp.concatenate([first[1], second[1]], axis=0),
    )


def fused_kernel(
    ns,
    nc,
    pieces,
    act_ref,
    proj_ref,
    taps_ref,
    filt_ref,
    cot_ref,
    table_ref,
    conv_ref,
    grad_ref,
    held_act,
    all_act,
    wide_in,
    part_sum,
    got_sum,
    far_got,
    conv_own,
    all_grad,
    part_grad,
    pair_grad,
    mirror_send,
    mirror_got,
    total_grad,
    turned,
    proj_v,
    proj_t,
    taps_v,
    table_v,
    send_sems,
    recv_sems,
    load_sems,
):
    s = lax.axis_index("seq")
    h = lax.axis_index("ch")
    rows = act_ref.shape[0]
    span = act_ref.shape[1]
    own = filt_ref.shape[0] // ns
    quarter = rows // nc
    piece = quarter // pieces
    length = span * ns
    partner = h + 1 - 2 * (h % 2)
    mirror = (h + nc // 2) % nc
    across = (partner + nc // 2) % nc
    started, loads = [], []

    @pl.when(s == 0)
    def _():
        got_sum[0] = jnp.zeros_like(got_sum[0])

    @pl.when(s == ns - 1)
    def _():
        got_sum[ns - 2] = jnp.zeros_like(got_sum[ns - 2])

    half = own // 2

    def block(index, size):
        return pl.ds(pl.multiple_of(index * size, size), size)

    def part(index, k):
        return pl.ds(pl.multiple_of(index * quarter + k * piece, piece), piece)

    def send(src, dst, when=None, into=None, **where):
        slot = len(started)
        into = slot if into is None else into
        copy = pltpu.make_async_remote_copy(
            src_ref=src,
            dst_ref=dst,
            send_sem=send_sems.at[slot],
            recv_sem=recv_sems.at[into],
            device_id=where,
            device_id_type=MESH,
        )
        if when is None:
            copy.start()
        else:
            pl.when(when)(lambda: copy.start())
        started.append((copy, when))
        return copy

    def load(src, dst):
        copy = pltpu.make_async_copy(src, dst, load_sems.at[len(loads)])
        copy.start()
        loads.append(copy)
        return copy

    barrier = pltpu.get_barrier_semaphore()
    for d in range(1, ns):
        pl.semaphore_signal(
            barrier, inc=1, device_id={"seq": (s + d) % ns}, device_id_type=MESH
        )
    for d in range(1, nc):
        pl.semaphore_signal(barrier, inc=1, device_id={"ch": (h + d) % nc}, device_id_type=MESH)
    act_own = load(act_ref.at[block(h, quarter), :], held_act.at[h])
    wide_own = [
        load(ref.at[block(s, own), :], wide_in.at[pl.ds(at * own, own), block(s, span)])
        for at, ref in enumerate((filt_ref, cot_ref))
    ]
    rest = [
        load(table_ref, table_v),
        load(taps_ref.at[block(s, own), :], taps_v),
        load(proj_ref, proj_v),
    ]
    pl.semaphore_wait(barrier, ns + nc - 2)

    spread = []
    for k in range(pieces):
        spread.append(
            [
                send(
                    act_ref.at[part((h + d) % nc, k), :],
                    held_act.at[h, pl.ds(k * piece, piece), :],
                    ch=(h + d) % nc,
                )
                for d in range(1, nc)
            ]
        )
    act_own.wait()
    moved = []
    for k in range(pieces):
        for copy in spread[k]:
            copy.wait_recv()
        moved.append(
            [
                send(
                    held_act.at[(s + d) % ns, pl.ds(k * piece, piece), :],
                    all_act.at[part(h, k), block(s, span)],
                    seq=(s + d) % ns,
                )
                for d in range(1, ns)
            ]
        )
    all_act[block(h, quarter), block(s, span)] = held_act[s]
    wide = []
    for at, ref in enumerate((filt_ref, cot_ref)):
        for d in range(1, ns):
            wide.append(
                send(
                    ref.at[block((s + d) % ns, own), :],
                    wide_in.at[pl.ds(at * own, own), block(s, span)],
                    seq=(s + d) % ns,
                )
            )
    shared, crossed = [], []
    for k in range(pieces):
        for copy in moved[k]:
            copy.wait_recv()
        crossed.append(send(all_act.at[part(h, k), :], all_act.at[part(h, k), :], ch=mirror))
        shared.append(send(all_act.at[part(h, k), :], all_act.at[part(h, k), :], ch=partner))

    for copy in rest:
        copy.wait()
    for at in range(ns):
        proj_t[pl.ds(at * own, own), :] = proj_v[:, pl.ds(at * own, own)].T
    for k in range(pieces):
        crossed[k].wait_recv()
        shared.append(
            send(all_act.at[part(mirror, k), :], all_act.at[part(mirror, k), :], ch=partner)
        )
    for copy in shared:
        copy.wait_recv()

    def half_of(index, c):
        return pl.ds(pl.multiple_of(index * own + c * half, half), half)

    inner = (s != 0) & (s != ns - 1)
    near = {1: s != ns - 1, 2: (s == 0) | (s == ns - 1), 3: s != 0}
    reduced, sum_slots, far = {}, {}, {}

    def sum_to(d, c):
        rows_to = half_of((s + d) % ns, c)
        at = pl.ds(c * half, half)
        if d != 2:
            far[c] = send(
                part_sum.at[rows_to, :],
                far_got.at[at, :],
                when=s == (ns - 1 if d == 1 else 0),
                into=sum_slots.setdefault(("far", c), len(started)),
                seq=ns - 2 if d == 1 else 1,
            )
        sum_slots[c, d] = len(started)
        reduced[c, d] = send(
            part_sum.at[rows_to, :],
            got_sum.at[d - 1, at, :],
            when=near[d],
            seq=(s + d) % ns,
        )

    for d in (3, 1, 2):
        got = jnp.dot(
            proj_t[block((s + d) % ns, own), :],
            all_act[...],
            preferred_element_type=jnp.float32,
        )
        part_sum[block((s + d) % ns, own), :] = got.astype(jnp.bfloat16)
        sum_to(d, 0)
    for d in (3, 1, 2):
        sum_to(d, 1)
    mixed = jnp.dot(
        proj_t[block(s, own), :], all_act[...], preferred_element_type=jnp.float32
    )
    for copy in wide_own:
        copy.wait()
    for copy in wide:
        copy.wait_recv()
    table = table_v[...]
    spec = to_spectrum(wide_in[...], table)
    filt = (spec[0][:own], spec[1][:own])
    cot = (spec[0][own:], spec[1][own:])
    taps_own = taps_v[...]
    taps_high = taps_own.astype(jnp.bfloat16)
    taps_low = (taps_own - taps_high.astype(jnp.float32)).astype(jnp.bfloat16)
    table_top = table_v[pl.ds(0, taps_own.shape[1]), :]
    high = to_spectrum(taps_high, table_top)
    low = to_spectrum(taps_low, table_top)
    taps = (high[0] + low[0], high[1] + low[1])
    back = from_spectrum(*times_conj(cot, filt), table).astype(jnp.bfloat16).astype(jnp.float32)

    for c in range(2):
        at = pl.ds(c * half, half)
        rows_to = half_of((s + 2) % ns, c)

        @pl.when(inner)
        def _(c=c, at=at, rows_to=rows_to):
            far[c].wait_recv()
            joined = part_sum[rows_to, :].astype(jnp.float32) + far_got[at, :].astype(jnp.float32)
            part_sum[rows_to, :] = joined.astype(jnp.bfloat16)

        send(
            part_sum.at[rows_to, :],
            got_sum.at[1, at, :],
            when=inner,
            into=sum_slots[c, 2],
            seq=(s + 2) % ns,
        )

    def place(p):
        return p % 2 * (ns // 2) + p // 2

    def stage_of(t, i):
        return block((t + 1 + i) % 2, length // 2)

    def relay(c):
        for i in range(2):
            gathered[c, i, 2].wait_recv()
            where = (half_of((s + 2) % ns, c), stage_of(s, i))
            for end, d in ((0, 1), (ns - 1, 3)):
                send(
                    all_grad.at[where],
                    all_grad.at[where],
                    when=s == (1 if end == 0 else ns - 2),
                    into=slots[c, 1 - i, d],
                    seq=end,
                )

    gathered, slots, mediums, gates = {}, {}, [], []
    for c in range(2):
        at = slice(c * half, (c + 1) * half)
        summed = mixed[at]
        for d in range(1, ns):
            if d == 2:
                reduced[c, d].wait_recv()
            else:
                pl.when(s != (0 if d == 1 else ns - 1))(reduced[c, d].wait_recv)
            summed = summed + got_sum[d - 1, pl.ds(c * half, half), :].astype(jnp.float32)
        values = summed.astype(jnp.bfloat16)
        gate = jax.nn.sigmoid(values.astype(jnp.float32))
        grad_medium = (back[at] * gate).astype(jnp.bfloat16)
        spec = to_spectrum(jnp.concatenate([values, grad_medium], axis=0), table)
        taps_half = (taps[0][at], taps[1][at])
        both = stacked(
            times((spec[0][:half], spec[1][:half]), taps_half),
            times_conj((spec[0][half:], spec[1][half:]), taps_half),
        )
        both = from_spectrum(*both, table)
        medium, through = both[:half], both[half:]
        grads = (through + back[at] * medium * gate * (1.0 - gate)).astype(jnp.bfloat16)
        for p in range(ns):
            all_grad[half_of(s, c), pl.ds(place(p) * span, span)] = grads[
                :, p * span : (p + 1) * span
            ]
        for i, d in [(0, 2), (1, 2), (0, 1), (0, 3), (1, 1), (1, 3)]:
            where = (half_of(s, c), stage_of((s + d) % ns, i))
            near = {1: s != ns - 1, 2: None, 3: s != 0}[d]
            slots[c, i, d] = len(started)
            gathered[c, i, d] = send(
                all_grad.at[where], all_grad.at[where], when=near, seq=(s + d) % ns
            )
        mediums.append(medium)
        gates.append(gate)
    medium, gate = jnp.concatenate(mediums, axis=0), jnp.concatenate(gates, axis=0)

    relay(0)
    gated = (medium * gate).astype(jnp.bfloat16)
    conv = from_spectrum(*times(to_spectrum(gated, table), filt), table)
    conv_own[...] = conv.astype(jnp.bfloat16)
    relay(1)
    returned = [
        send(
            conv_own.at[:, block((s + d) % ns, span)],
            conv_ref.at[block(s, own), :],
            seq=(s + d) % ns,
        )
        for d in range(1, ns)
    ]
    kept_out = [load(conv_own.at[:, block(s, span)], conv_ref.at[block(s, own), :])]

    def partial(to, i):
        return jnp.dot(
            proj_v[block(to, quarter), :],
            all_grad[:, stage_of(s, i)],
            preferred_element_type=jnp.float32,
        )

    seconds, mirrored = [], []
    for i in range(2):
        lanes = stage_of(s, i)
        for c, d in ((0, 1), (0, 3), (1, 1), (1, 3)):
            gathered[c, i, d].wait_recv()
        pair = []
        for side, to in enumerate((across, partner)):
            part_grad[block(to, quarter), lanes] = partial(to, i).astype(jnp.bfloat16)
            pair.append(
                send(
                    part_grad.at[block(to, quarter), lanes],
                    pair_grad.at[side, :, lanes],
                    ch=partner,
                )
            )
        kept = partial(mirror, i)
        pair[0].wait_recv()
        kept = kept + pair_grad[0, :, lanes].astype(jnp.float32)
        mirror_send[:, lanes] = kept.astype(jnp.bfloat16)
        copies = []
        for k in range(pieces):
            at = pl.ds(k * piece, piece)
            copies.append(send(mirror_send.at[at, lanes], mirror_got.at[at, lanes], ch=mirror))
        seconds.append(pair[1])
        mirrored.append(copies)
    placed = [[] for _ in range(pieces)]
    for i in range(2):
        lanes = stage_of(s, i)
        kept = partial(h, i)
        seconds[i].wait_recv()
        for k in range(pieces):
            at = pl.ds(k * piece, piece)
            some = kept[k * piece : (k + 1) * piece] + pair_grad[1, at, lanes].astype(jnp.float32)
            mirrored[i][k].wait_recv()
            some = some + mirror_got[at, lanes].astype(jnp.float32)
            total_grad[at, lanes] = some.astype(jnp.bfloat16)
            for d in range(1, ns):
                if (d + 1 + i) % 2 == 0:
                    to = (s + d) % ns
                    placed[k].append(
                        send(
                            total_grad.at[at, block(place(to), span)],
                            turned.at[s, at, :],
                            seq=to,
                        )
                    )
            if i == 1:
                turned[s, at, :] = total_grad[at, block(place(s), span)]
    final = []
    for k in range(pieces):
        at = pl.ds(k * piece, piece)
        for copy in placed[k]:
            copy.wait_recv()
        final += [
            send(turned.at[(h + d) % nc, at, :], grad_ref.at[part(h, k), :], ch=(h + d) % nc)
            for d in range(1, nc)
        ]
        kept_out.append(load(turned.at[h, at, :], grad_ref.at[part(h, k), :]))
    for copy in returned:
        copy.wait_recv()
    for copy in final:
        copy.wait_recv()
    for copy in kept_out:
        copy.wait()
    for copy, when in started:
        if when is None:
            copy.wait_send()
        else:
            pl.when(when)(lambda copy=copy: copy.wait_send())


def fused_on_device(ns, nc, activations, projection, medium_taps, long_filters, cotangent):
    rows, span = activations.shape
    channels = long_filters.shape[0]
    own = channels // ns
    taps = medium_taps.shape[1]
    length = span * ns
    quarter = rows // nc
    pieces = 2
    copies = 9 * pieces + 3 * pieces + 3 * pieces + 6 * pieces + 24 + 40
    hbm = pl.BlockSpec(memory_space=pltpu.HBM)
    bf16 = jnp.bfloat16
    return pl.pallas_call(
        functools.partial(fused_kernel, ns, nc, pieces),
        out_shape=(
            jax.ShapeDtypeStruct((channels, span), bf16),
            jax.ShapeDtypeStruct((rows, span), bf16),
        ),
        in_specs=[hbm] * 6,
        out_specs=(hbm, hbm),
        scratch_shapes=[
            pltpu.VMEM((nc, quarter, span), bf16),
            pltpu.VMEM((rows, length), bf16),
            pltpu.VMEM((2 * own, length), bf16),
            pltpu.VMEM((channels, length), bf16),
            pltpu.VMEM((ns - 1, own, length), bf16),
            pltpu.VMEM((own, length), bf16),
            pltpu.VMEM((own, length), bf16),
            pltpu.VMEM((channels, length), bf16),
            pltpu.VMEM((rows, length), bf16),
            pltpu.VMEM((2, quarter, length), bf16),
            pltpu.VMEM((quarter, length), bf16),
            pltpu.VMEM((quarter, length), bf16),
            pltpu.VMEM((quarter, length), bf16),
            pltpu.VMEM((ns, quarter, span), bf16),
            pltpu.VMEM((rows, channels), bf16),
            pltpu.VMEM((channels, rows), bf16),
            pltpu.VMEM((own, taps), jnp.float32),
            pltpu.VMEM((length, 2 * length), bf16),
            pltpu.SemaphoreType.DMA((copies,)),
            pltpu.SemaphoreType.DMA((copies,)),
            pltpu.SemaphoreType.DMA((16,)),
        ],
        compiler_params=pltpu.CompilerParams(
            collective_id=0, has_side_effects=True, vmem_limit_bytes=60 * 1024 * 1024
        ),
    )(activations, projection, medium_taps, long_filters, cotangent, transform_table(length))


def solution(mesh):
    ns, nc = mesh.shape["seq"], mesh.shape["ch"]

    def on_any(activations, projection, medium_taps, long_filters, cotangent):
        arrays = (activations, projection, medium_taps, long_filters, cotangent)
        table_bytes = 4 * (activations.shape[1] * ns) ** 2
        if ns == nc == 4 and table_bytes <= 4 << 20:
            return fused_on_device(ns, nc, *arrays)
        return on_device(*arrays)

    return jax.shard_map(
        on_any,
        mesh=mesh,
        in_specs=(
            P("ch", ("grp", "seq")),
            P("seq", "ch"),
            P("ch", None),
            P("ch", "seq"),
            P("ch", ("grp", "seq")),
        ),
        out_specs=(P("ch", ("grp", "seq")), P("ch", ("grp", "seq"))),
        check_vma=False,
    )
```

```python
import functools
import math

import jax
import jax.numpy as jnp
import numpy as np
from jax import lax
from jax.experimental import pallas as pl
from jax.experimental.pallas import tpu as pltpu
from jax.sharding import PartitionSpec as P

exact_mode = lax.Precision.HIGH


def medium_forward(padded, tap_weights, length):
    tap_count = tap_weights.shape[1]
    summed = jnp.zeros((padded.shape[0], length), jnp.float32)
    for offset in range(tap_count):
        begin_col = tap_count - 1 - offset
        summed = (
            summed + tap_weights[:, offset : offset + 1] * padded[:, begin_col : begin_col + length]
        )
    return summed


def medium_backward(padded, tap_weights, length):
    tap_count = tap_weights.shape[1]
    summed = jnp.zeros((padded.shape[0], length), jnp.float32)
    for offset in range(tap_count):
        summed = summed + tap_weights[:, offset : offset + 1] * padded[:, offset : offset + length]
    return summed


def dft_tables(length):
    points = 2 * length
    columns = 128
    row_count = points // columns
    half_rows = row_count // 2
    freq_rows = jnp.arange(row_count, dtype=jnp.int32)
    time_rows = jnp.arange(half_rows, dtype=jnp.int32)
    lane_index = jnp.arange(columns, dtype=jnp.int32)
    angle_first = (
        2.0
        * math.pi
        / row_count
        * (freq_rows[:, None] * time_rows[None, :] % row_count).astype(jnp.float32)
    )
    angle_twist = (
        2.0
        * math.pi
        / points
        * (freq_rows[:, None] * lane_index[None, :] % points).astype(jnp.float32)
    )
    angle_last = (
        2.0
        * math.pi
        / columns
        * (lane_index[:, None] * lane_index[None, :] % columns).astype(jnp.float32)
    )
    return (
        jnp.cos(angle_first),
        jnp.sin(angle_first),
        jnp.cos(angle_twist),
        jnp.sin(angle_twist),
        jnp.cos(angle_last),
        jnp.sin(angle_last),
    )


def forward_dft(signal, tables):
    cos_first, sin_first, cos_twist, sin_twist, cos_last, sin_last = tables
    channels = signal.shape[0]
    shaped = signal.reshape(channels, cos_first.shape[1], 128)
    section_re = jnp.einsum("kn,cnq->ckq", cos_first, shaped, precision=exact_mode)
    section_im = -jnp.einsum("kn,cnq->ckq", sin_first, shaped, precision=exact_mode)
    twist_re = section_re * cos_twist + section_im * sin_twist
    twist_im = section_im * cos_twist - section_re * sin_twist
    spec_re = jnp.einsum("ckq,qm->ckm", twist_re, cos_last, precision=exact_mode) + jnp.einsum(
        "ckq,qm->ckm", twist_im, sin_last, precision=exact_mode
    )
    spec_im = jnp.einsum("ckq,qm->ckm", twist_im, cos_last, precision=exact_mode) - jnp.einsum(
        "ckq,qm->ckm", twist_re, sin_last, precision=exact_mode
    )
    return (spec_re, spec_im)


def inverse_dft(spec_re, spec_im, tables):
    cos_first, sin_first, cos_twist, sin_twist, cos_last, sin_last = tables
    channels = spec_re.shape[0]
    half_rows = cos_first.shape[1]
    inner_re = jnp.einsum("ckq,qm->ckm", spec_re, cos_last, precision=exact_mode) - jnp.einsum(
        "ckq,qm->ckm", spec_im, sin_last, precision=exact_mode
    )
    inner_im = jnp.einsum("ckq,qm->ckm", spec_im, cos_last, precision=exact_mode) + jnp.einsum(
        "ckq,qm->ckm", spec_re, sin_last, precision=exact_mode
    )
    turned_re = inner_re * cos_twist - inner_im * sin_twist
    turned_im = inner_im * cos_twist + inner_re * sin_twist
    output = jnp.einsum("kn,ckq->cnq", cos_first, turned_re, precision=exact_mode) - jnp.einsum(
        "kn,ckq->cnq", sin_first, turned_im, precision=exact_mode
    )
    points = 2 * half_rows * 128
    return (output / points).reshape(channels, half_rows * 128)


def causal_apply(signal, filt_re, filt_im, tables, conjugate):
    sig_re, sig_im = forward_dft(signal, tables)
    if conjugate:
        prod_re = sig_re * filt_re + sig_im * filt_im
        prod_im = sig_im * filt_re - sig_re * filt_im
    else:
        prod_re = sig_re * filt_re - sig_im * filt_im
        prod_im = sig_im * filt_re + sig_re * filt_im
    return inverse_dft(prod_re, prod_im, tables)


def on_device(activations, projection, medium_taps, long_filters, cotangent):
    tap_count = medium_taps.shape[1]
    whole_in = lax.all_gather(activations, "ch", axis=0, tiled=True)
    mixed_sum = lax.dot_general(
        lax.all_gather(projection, "seq", axis=0, tiled=True),
        whole_in,
        (((0,), (0,)), ((), ())),
        preferred_element_type=jnp.float32,
    )
    values = mixed_sum.astype(jnp.bfloat16)
    channel_count = values.shape[0] // lax.axis_size("seq")
    own_taps = lax.dynamic_slice_in_dim(
        medium_taps, lax.axis_index("seq") * channel_count, channel_count, 0
    )
    arrived, filters_ch = (
        lax.all_to_all(values, "seq", split_axis=0, concat_axis=1, tiled=True),
        lax.all_to_all(long_filters, "seq", split_axis=0, concat_axis=1, tiled=True),
    )
    tables = dft_tables(arrived.shape[1])
    filt_re, filt_im = forward_dft(filters_ch.astype(jnp.float32), tables)
    values_ch = arrived.astype(jnp.float32)
    padded_ch = jnp.pad(values_ch, ((0, 0), (tap_count - 1, 0)))
    conv_ch = medium_forward(padded_ch, own_taps, arrived.shape[1])
    gate_ch = jax.nn.sigmoid(values_ch)
    signal = lax.optimization_barrier((conv_ch * gate_ch).astype(jnp.bfloat16)).astype(jnp.float32)
    kept_state = (conv_ch, gate_ch)
    output_ch = causal_apply(signal, filt_re, filt_im, tables, False).astype(jnp.bfloat16)
    output_ch, context = (output_ch, (filt_re, filt_im, tables, kept_state))
    conv_out = lax.all_to_all(output_ch, "seq", split_axis=1, concat_axis=0, tiled=True)
    grad_ch = lax.all_to_all(cotangent, "seq", split_axis=0, concat_axis=1, tiled=True)
    filt_re, filt_im, tables, kept_state = context
    back_grad = lax.optimization_barrier(
        causal_apply(grad_ch.astype(jnp.float32), filt_re, filt_im, tables, True).astype(
            jnp.bfloat16
        )
    )
    conv_ch, gate_ch = kept_state
    grad_wide = back_grad.astype(jnp.float32)
    conv_grad = lax.optimization_barrier((grad_wide * gate_ch).astype(jnp.bfloat16)).astype(
        jnp.float32
    )
    padded_grad = jnp.pad(conv_grad, ((0, 0), (0, tap_count - 1)))
    through = medium_backward(padded_grad, own_taps, conv_grad.shape[1])
    gate_grad = grad_wide * conv_ch * gate_ch * (1.0 - gate_ch)
    back_ch = (through + gate_grad).astype(jnp.bfloat16)
    returned = lax.all_to_all(back_ch, "seq", split_axis=1, concat_axis=0, tiled=True)
    partial_grad = jnp.dot(
        lax.all_gather(projection, "seq", axis=0, tiled=True),
        returned,
        preferred_element_type=jnp.float32,
    )
    input_grad = lax.psum_scatter(
        partial_grad.astype(jnp.bfloat16), "ch", scatter_dimension=0, tiled=True
    )
    return (conv_out, input_grad)


MESH = pl.DeviceIdType.MESH


def transform_table(length):
    points = 2 * length
    turns = np.arange(length)[:, None] * (2 * np.arange(length)[None, :] + 1) % (2 * points)
    angles = turns * (math.pi / points)
    return jnp.asarray(np.concatenate([np.cos(angles), np.sin(angles)], axis=1), jnp.bfloat16)


def to_spectrum(signal, table):
    spectrum = jnp.dot(signal, table, preferred_element_type=jnp.float32)
    half = spectrum.shape[1] // 2
    return spectrum[:, :half], spectrum[:, half:]


def from_spectrum(even, odd, table):
    both = jnp.concatenate([even, odd], axis=1).astype(jnp.bfloat16)
    signal = lax.dot_general(
        both, table, (((1,), (1,)), ((), ())), preferred_element_type=jnp.float32
    )
    return signal * (1.0 / table.shape[0])


def times(left, right):
    return left[0] * right[0] - left[1] * right[1], left[0] * right[1] + left[1] * right[0]


def times_conj(left, right):
    return left[0] * right[0] + left[1] * right[1], left[1] * right[0] - left[0] * right[1]


def stacked(first, second):
    return (
        jnp.concatenate([first[0], second[0]], axis=0),
        jnp.concatenate([first[1], second[1]], axis=0),
    )


def fused_kernel(
    ns,
    nc,
    pieces,
    act_ref,
    proj_ref,
    taps_ref,
    filt_ref,
    cot_ref,
    table_ref,
    conv_ref,
    grad_ref,
    held_act,
    all_act,
    wide_in,
    part_sum,
    got_sum,
    far_got,
    conv_own,
    all_grad,
    part_grad,
    pair_grad,
    mirror_send,
    mirror_got,
    total_grad,
    turned,
    proj_v,
    proj_t,
    taps_v,
    table_v,
    send_sems,
    recv_sems,
    load_sems,
):
    s = lax.axis_index("seq")
    h = lax.axis_index("ch")
    rows = act_ref.shape[0]
    span = act_ref.shape[1]
    own = filt_ref.shape[0] // ns
    quarter = rows // nc
    piece = quarter // pieces
    length = span * ns
    partner = h + 1 - 2 * (h % 2)
    mirror = (h + nc // 2) % nc
    across = (partner + nc // 2) % nc
    started, loads = [], []

    @pl.when(s == 0)
    def _():
        got_sum[0] = jnp.zeros_like(got_sum[0])

    @pl.when(s == ns - 1)
    def _():
        got_sum[ns - 2] = jnp.zeros_like(got_sum[ns - 2])

    half = own // 2

    def block(index, size):
        return pl.ds(pl.multiple_of(index * size, size), size)

    def part(index, k):
        return pl.ds(pl.multiple_of(index * quarter + k * piece, piece), piece)

    def send(src, dst, when=None, into=None, **where):
        slot = len(started)
        into = slot if into is None else into
        copy = pltpu.make_async_remote_copy(
            src_ref=src,
            dst_ref=dst,
            send_sem=send_sems.at[slot],
            recv_sem=recv_sems.at[into],
            device_id=where,
            device_id_type=MESH,
        )
        if when is None:
            copy.start()
        else:
            pl.when(when)(lambda: copy.start())
        started.append((copy, when))
        return copy

    def load(src, dst):
        copy = pltpu.make_async_copy(src, dst, load_sems.at[len(loads)])
        copy.start()
        loads.append(copy)
        return copy

    barrier = pltpu.get_barrier_semaphore()
    for d in range(1, ns):
        pl.semaphore_signal(
            barrier, inc=1, device_id={"seq": (s + d) % ns}, device_id_type=MESH
        )
    for d in range(1, nc):
        pl.semaphore_signal(barrier, inc=1, device_id={"ch": (h + d) % nc}, device_id_type=MESH)
    act_own = load(act_ref.at[block(h, quarter), :], held_act.at[h])
    wide_own = [
        load(ref.at[block(s, own), :], wide_in.at[pl.ds(at * own, own), block(s, span)])
        for at, ref in enumerate((filt_ref, cot_ref))
    ]
    rest = [
        load(table_ref, table_v),
        load(taps_ref.at[block(s, own), :], taps_v),
        load(proj_ref, proj_v),
    ]
    pl.semaphore_wait(barrier, ns + nc - 2)

    spread = []
    for k in range(pieces):
        spread.append(
            [
                send(
                    act_ref.at[part((h + d) % nc, k), :],
                    held_act.at[h, pl.ds(k * piece, piece), :],
                    ch=(h + d) % nc,
                )
                for d in range(1, nc)
            ]
        )
    act_own.wait()
    wide = []

    def widen(at, ref):
        for d in range(1, ns):
            wide.append(
                send(
                    ref.at[block((s + d) % ns, own), :],
                    wide_in.at[pl.ds(at * own, own), block(s, span)],
                    seq=(s + d) % ns,
                )
            )

    widen(0, filt_ref)
    moved = []
    for k in range(pieces):
        for copy in spread[k]:
            copy.wait_recv()
        moved.append(
            [
                send(
                    held_act.at[(s + d) % ns, pl.ds(k * piece, piece), :],
                    all_act.at[part(h, k), block(s, span)],
                    seq=(s + d) % ns,
                )
                for d in range(1, ns)
            ]
        )
    all_act[block(h, quarter), block(s, span)] = held_act[s]
    widen(1, cot_ref)
    shared, crossed = [], []
    for k in range(pieces):
        for copy in moved[k]:
            copy.wait_recv()
        crossed.append(send(all_act.at[part(h, k), :], all_act.at[part(h, k), :], ch=mirror))
        shared.append(send(all_act.at[part(h, k), :], all_act.at[part(h, k), :], ch=partner))

    for copy in rest:
        copy.wait()
    for at in range(ns):
        proj_t[pl.ds(at * own, own), :] = proj_v[:, pl.ds(at * own, own)].T
    for k in range(pieces):
        crossed[k].wait_recv()
        shared.append(
            send(all_act.at[part(mirror, k), :], all_act.at[part(mirror, k), :], ch=partner)
        )
    for copy in shared:
        copy.wait_recv()

    def half_of(index, c):
        return pl.ds(pl.multiple_of(index * own + c * half, half), half)

    inner = (s != 0) & (s != ns - 1)
    near = {1: s != ns - 1, 2: (s == 0) | (s == ns - 1), 3: s != 0}
    reduced, sum_slots, far = {}, {}, {}

    def sum_to(d, c):
        rows_to = half_of((s + d) % ns, c)
        at = pl.ds(c * half, half)
        if d != 2:
            far[c] = send(
                part_sum.at[rows_to, :],
                far_got.at[at, :],
                when=s == (ns - 1 if d == 1 else 0),
                into=sum_slots.setdefault(("far", c), len(started)),
                seq=ns - 2 if d == 1 else 1,
            )
        sum_slots[c, d] = len(started)
        reduced[c, d] = send(
            part_sum.at[rows_to, :],
            got_sum.at[d - 1, at, :],
            when=near[d],
            seq=(s + d) % ns,
        )

    for d in (3, 1, 2):
        got = jnp.dot(
            proj_t[block((s + d) % ns, own), :],
            all_act[...],
            preferred_element_type=jnp.float32,
        )
        part_sum[block((s + d) % ns, own), :] = got.astype(jnp.bfloat16)
        sum_to(d, 0)
    for d in (3, 1, 2):
        sum_to(d, 1)
    mixed = jnp.dot(
        proj_t[block(s, own), :], all_act[...], preferred_element_type=jnp.float32
    )
    for copy in wide_own:
        copy.wait()
    for copy in wide:
        copy.wait_recv()
    table = table_v[...]
    spec = to_spectrum(wide_in[...], table)
    filt = (spec[0][:own], spec[1][:own])
    cot = (spec[0][own:], spec[1][own:])
    taps_own = taps_v[...]
    taps_high = taps_own.astype(jnp.bfloat16)
    taps_low = (taps_own - taps_high.astype(jnp.float32)).astype(jnp.bfloat16)
    table_top = table_v[pl.ds(0, taps_own.shape[1]), :]
    high = to_spectrum(taps_high, table_top)
    low = to_spectrum(taps_low, table_top)
    taps = (high[0] + low[0], high[1] + low[1])
    back = from_spectrum(*times_conj(cot, filt), table).astype(jnp.bfloat16).astype(jnp.float32)

    for c in range(2):
        at = pl.ds(c * half, half)
        rows_to = half_of((s + 2) % ns, c)

        @pl.when(inner)
        def _(c=c, at=at, rows_to=rows_to):
            far[c].wait_recv()
            joined = part_sum[rows_to, :].astype(jnp.float32) + far_got[at, :].astype(jnp.float32)
            part_sum[rows_to, :] = joined.astype(jnp.bfloat16)

        send(
            part_sum.at[rows_to, :],
            got_sum.at[1, at, :],
            when=inner,
            into=sum_slots[c, 2],
            seq=(s + 2) % ns,
        )

    def place(p):
        return p % 2 * (ns // 2) + p // 2

    def stage_of(t, i):
        return block((t + 1 + i) % 2, length // 2)

    def relay(c):
        for i in range(2):
            gathered[c, i, 2].wait_recv()
            where = (half_of((s + 2) % ns, c), stage_of(s, i))
            for end, d in ((0, 1), (ns - 1, 3)):
                send(
                    all_grad.at[where],
                    all_grad.at[where],
                    when=s == (1 if end == 0 else ns - 2),
                    into=slots[c, 1 - i, d],
                    seq=end,
                )

    gathered, slots, mediums, gates = {}, {}, [], []
    for c in range(2):
        at = slice(c * half, (c + 1) * half)
        summed = mixed[at]
        for d in range(1, ns):
            if d == 2:
                reduced[c, d].wait_recv()
            else:
                pl.when(s != (0 if d == 1 else ns - 1))(reduced[c, d].wait_recv)
            summed = summed + got_sum[d - 1, pl.ds(c * half, half), :].astype(jnp.float32)
        values = summed.astype(jnp.bfloat16)
        gate = jax.nn.sigmoid(values.astype(jnp.float32))
        grad_medium = (back[at] * gate).astype(jnp.bfloat16)
        spec = to_spectrum(jnp.concatenate([values, grad_medium], axis=0), table)
        taps_half = (taps[0][at], taps[1][at])
        both = stacked(
            times((spec[0][:half], spec[1][:half]), taps_half),
            times_conj((spec[0][half:], spec[1][half:]), taps_half),
        )
        both = from_spectrum(*both, table)
        medium, through = both[:half], both[half:]
        grads = (through + back[at] * medium * gate * (1.0 - gate)).astype(jnp.bfloat16)
        for p in range(ns):
            all_grad[half_of(s, c), pl.ds(place(p) * span, span)] = grads[
                :, p * span : (p + 1) * span
            ]
        for i, d in [(0, 2), (1, 2), (0, 1), (0, 3), (1, 1), (1, 3)]:
            where = (half_of(s, c), stage_of((s + d) % ns, i))
            near = {1: s != ns - 1, 2: None, 3: s != 0}[d]
            slots[c, i, d] = len(started)
            gathered[c, i, d] = send(
                all_grad.at[where], all_grad.at[where], when=near, seq=(s + d) % ns
            )
        mediums.append(medium)
        gates.append(gate)
    medium, gate = jnp.concatenate(mediums, axis=0), jnp.concatenate(gates, axis=0)

    relay(0)
    gated = (medium * gate).astype(jnp.bfloat16)
    conv = from_spectrum(*times(to_spectrum(gated, table), filt), table)
    conv_own[...] = conv.astype(jnp.bfloat16)
    relay(1)
    returned = [
        send(
            conv_own.at[:, block((s + d) % ns, span)],
            conv_ref.at[block(s, own), :],
            seq=(s + d) % ns,
        )
        for d in range(1, ns)
    ]
    kept_out = [load(conv_own.at[:, block(s, span)], conv_ref.at[block(s, own), :])]

    def partial(to, i):
        return jnp.dot(
            proj_v[block(to, quarter), :],
            all_grad[:, stage_of(s, i)],
            preferred_element_type=jnp.float32,
        )

    seconds, mirrored = [], []
    for i in range(2):
        lanes = stage_of(s, i)
        for c, d in ((0, 1), (0, 3), (1, 1), (1, 3)):
            gathered[c, i, d].wait_recv()
        pair = []
        for side, to in enumerate((across, partner)):
            part_grad[block(to, quarter), lanes] = partial(to, i).astype(jnp.bfloat16)
            pair.append(
                send(
                    part_grad.at[block(to, quarter), lanes],
                    pair_grad.at[side, :, lanes],
                    ch=partner,
                )
            )
        kept = partial(mirror, i)
        pair[0].wait_recv()
        kept = kept + pair_grad[0, :, lanes].astype(jnp.float32)
        mirror_send[:, lanes] = kept.astype(jnp.bfloat16)
        copies = []
        for k in range(pieces):
            at = pl.ds(k * piece, piece)
            copies.append(send(mirror_send.at[at, lanes], mirror_got.at[at, lanes], ch=mirror))
        seconds.append(pair[1])
        mirrored.append(copies)
    placed = [[] for _ in range(pieces)]
    for i in range(2):
        lanes = stage_of(s, i)
        kept = partial(h, i)
        seconds[i].wait_recv()
        for k in range(pieces):
            at = pl.ds(k * piece, piece)
            some = kept[k * piece : (k + 1) * piece] + pair_grad[1, at, lanes].astype(jnp.float32)
            mirrored[i][k].wait_recv()
            some = some + mirror_got[at, lanes].astype(jnp.float32)
            total_grad[at, lanes] = some.astype(jnp.bfloat16)
            for d in range(1, ns):
                if (d + 1 + i) % 2 == 0:
                    to = (s + d) % ns
                    placed[k].append(
                        send(
                            total_grad.at[at, block(place(to), span)],
                            turned.at[s, at, :],
                            seq=to,
                        )
                    )
            if i == 1:
                turned[s, at, :] = total_grad[at, block(place(s), span)]
    final = []
    for k in range(pieces):
        at = pl.ds(k * piece, piece)
        for copy in placed[k]:
            copy.wait_recv()
        final += [
            send(turned.at[(h + d) % nc, at, :], grad_ref.at[part(h, k), :], ch=(h + d) % nc)
            for d in range(1, nc)
        ]
        kept_out.append(load(turned.at[h, at, :], grad_ref.at[part(h, k), :]))
    for copy in returned:
        copy.wait_recv()
    for copy in final:
        copy.wait_recv()
    for copy in kept_out:
        copy.wait()
    for copy, when in started:
        if when is None:
            copy.wait_send()
        else:
            pl.when(when)(lambda copy=copy: copy.wait_send())


def fused_on_device(ns, nc, activations, projection, medium_taps, long_filters, cotangent):
    rows, span = activations.shape
    channels = long_filters.shape[0]
    own = channels // ns
    taps = medium_taps.shape[1]
    length = span * ns
    quarter = rows // nc
    pieces = 2
    copies = 9 * pieces + 3 * pieces + 3 * pieces + 6 * pieces + 24 + 40
    hbm = pl.BlockSpec(memory_space=pltpu.HBM)
    bf16 = jnp.bfloat16
    return pl.pallas_call(
        functools.partial(fused_kernel, ns, nc, pieces),
        out_shape=(
            jax.ShapeDtypeStruct((channels, span), bf16),
            jax.ShapeDtypeStruct((rows, span), bf16),
        ),
        in_specs=[hbm] * 6,
        out_specs=(hbm, hbm),
        scratch_shapes=[
            pltpu.VMEM((nc, quarter, span), bf16),
            pltpu.VMEM((rows, length), bf16),
            pltpu.VMEM((2 * own, length), bf16),
            pltpu.VMEM((channels, length), bf16),
            pltpu.VMEM((ns - 1, own, length), bf16),
            pltpu.VMEM((own, length), bf16),
            pltpu.VMEM((own, length), bf16),
            pltpu.VMEM((channels, length), bf16),
            pltpu.VMEM((rows, length), bf16),
            pltpu.VMEM((2, quarter, length), bf16),
            pltpu.VMEM((quarter, length), bf16),
            pltpu.VMEM((quarter, length), bf16),
            pltpu.VMEM((quarter, length), bf16),
            pltpu.VMEM((ns, quarter, span), bf16),
            pltpu.VMEM((rows, channels), bf16),
            pltpu.VMEM((channels, rows), bf16),
            pltpu.VMEM((own, taps), jnp.float32),
            pltpu.VMEM((length, 2 * length), bf16),
            pltpu.SemaphoreType.DMA((copies,)),
            pltpu.SemaphoreType.DMA((copies,)),
            pltpu.SemaphoreType.DMA((16,)),
        ],
        compiler_params=pltpu.CompilerParams(
            collective_id=0, has_side_effects=True, vmem_limit_bytes=60 * 1024 * 1024
        ),
    )(activations, projection, medium_taps, long_filters, cotangent, transform_table(length))


def solution(mesh):
    ns, nc = mesh.shape["seq"], mesh.shape["ch"]

    def on_any(activations, projection, medium_taps, long_filters, cotangent):
        arrays = (activations, projection, medium_taps, long_filters, cotangent)
        table_bytes = 4 * (activations.shape[1] * ns) ** 2
        if ns == nc == 4 and table_bytes <= 4 << 20:
            return fused_on_device(ns, nc, *arrays)
        return on_device(*arrays)

    return jax.shard_map(
        on_any,
        mesh=mesh,
        in_specs=(
            P("ch", ("grp", "seq")),
            P("seq", "ch"),
            P("ch", None),
            P("ch", "seq"),
            P("ch", ("grp", "seq")),
        ),
        out_specs=(P("ch", ("grp", "seq")), P("ch", ("grp", "seq"))),
        check_vma=False,
    )
```
